32 devices in a mesh: group: 2 (over x), surf: 16 (over z, y, core).
Axes of the slice: x: 2, y: 2, z: 4, core: 2. Of those that a mesh axis runs over, the one named last changes fastest.
Arguments:
- traces: bfloat16 [4096, 128, 1024], P('surf', 'group'), parts along dimension 1, may hold values from -6 to 6
- operator: bfloat16 [4096, 8, 2, 4096], P('surf'), may hold values from -1 to 1, as said below
- freq_bins: int32 [8], replicated, may hold values from 1 to 511, as said below
- win_lengths: int32 [16], replicated, may hold values from 1 to 96, 1024 in all
- coefficients: float32 [16, 31], replicated, may hold values from -2.5 to 2.5
- neighbour: int32 [4096], P('surf'), may hold values from -2 to 2, as said below
Outputs:
- demultiple: bfloat16 [4096, 128, 1024], P('surf', 'group'), parts along dimension 1
The draws below stay inside these ranges and needn't reach their ends.
There are 2 independent parts, one for each index of `group`. The reference program is written for one: setup_inputs(seed, part) draws one part's arguments, and reference() takes and returns one part's arrays. A program takes and returns all parts, laid end to end along the dimension named above; an argument that names none is the same for every part. Nothing has to cross between parts.
Inputs may be any that keep to these rules, and one draw needn't show every extreme that they name: operator[i, f, c, j] equals operator[j, f, c, i] (reciprocity). `freq_bins`: the 8 bins are distinct. `neighbour`: points of even index take an offset of -2 or -1, points of odd index 1 or 2.
All inputs are finite; a program needn't handle non-finite values.
Results may differ from the reference program's by a relative error of at most 0.004.
Values may be sent and summed in bfloat16 or wider, within the bound.
A program may use at most 192 MiB of HBM per device.

```python
import math
import jax
import jax.numpy as jnp
import numpy as np
from jax import lax

NPTS = 4096
F = 8
NT = 1024
SHOTS = 64
TAPS = 31
HALO = 2
NWIN = 16


def draw_operator(key, part):
    values = jax.random.uniform(key, (NPTS, F, 2, NPTS), jnp.float32, -1.0, 1.0)
    mirrored = 0.5 * (values + jnp.transpose(values, (3, 1, 2, 0)))
    return (mirrored * (3.0 / NPTS) ** 0.5).astype(jnp.bfloat16)


def draw_freq_bins(key, part):
    return (jax.random.permutation(key, NT // 2 - 1)[:F] + 1).astype(jnp.int32)


def draw_neighbour(key, part):
    reach = jax.random.randint(key, (NPTS,), 1, 3, jnp.int32)
    parity = jnp.arange(NPTS, dtype=jnp.int32) % 2
    return (reach * (2 * parity - 1)).astype(jnp.int32)


def level_of(stream_key, shape, split, smallest, top_value):
    loudness = 1.0
    for dim, blocks in split:
        heights = jax.random.uniform(jax.random.fold_in(jax.random.fold_in(stream_key, 6), dim), (blocks,), jnp.float32, smallest / len(split), top_value / len(split))
        loudness = loudness * jnp.repeat(jnp.exp(heights), shape[dim] // blocks).reshape((-1,) + (1,) * (len(shape) - 1 - dim))
    return loudness


def profile(count, total, most, slope):
    portions = [(1 << 20) // math.isqrt(grade ** slope) + 1 for grade in range(2, count + 1)]
    rest, given = total - most - (count - 1), [1] * (count - 1)
    while rest > 0:
        movable = [i for i in range(count - 1) if given[i] < most]
        pool, left = sum([portions[i] for i in movable]), rest
        for i in movable:
            more = min(most - given[i], max(1, left * portions[i] // pool), rest)
            given[i] = given[i] + more
            rest = rest - more
    return np.array([most] + given)


def ragged(rng, amount, total, most, slope):
    if amount == 2:
        one = jax.random.randint(rng, (), max(1, total - most), min(most, total - 1) + 1)
        return jnp.stack([one, total - one])
    tallies = jnp.asarray(profile(amount, total, most, slope), jnp.int32)
    twos = (amount - 1) // 2
    giver, taker = tallies[1:1 + 2 * twos:2], tallies[2:2 + 2 * twos:2]
    margin = jnp.minimum(giver - 1, most - taker)
    moved = jax.random.randint(jax.random.fold_in(rng, 1), (twos,), 0, 1 << 20) % (margin + 1)
    tallies = tallies.at[1:1 + 2 * twos:2].set(giver - moved).at[2:2 + 2 * twos:2].set(taker + moved)
    return tallies[jax.random.permutation(jax.random.fold_in(rng, 2), amount)]


def gaussian(own_key, shape, spread, bound, shards=(), kind=jnp.bfloat16):
    array = jax.random.normal(own_key, shape, jnp.float32) * spread
    if len(shards) > 0:
        array = level_of(own_key, shape, shards, -0.22, 0.18) * array
    return jnp.clip(array, min=-bound, max=bound).astype(kind)


def setup_inputs(seed: int = 0, part: int = 0) -> dict:
    splits = jax.random.split(jax.random.key(seed), 7)
    own_keys = jax.random.split(jax.random.fold_in(splits[6], part), 7)
    traces = gaussian(own_keys[0], (NPTS, SHOTS, NT), 1.0, 6.0, ((0, 16),))
    operator = draw_operator(jax.random.fold_in(splits[6], 71), part)
    freq_bins = draw_freq_bins(jax.random.fold_in(splits[6], 71), part)
    win_lengths = ragged(splits[3], NWIN, NT, NT * 3 // (2 * NWIN), 0).astype(jnp.int32)
    coefficients = gaussian(splits[4], (NWIN, TAPS), 0.18, 2.5, (), jnp.float32)
    neighbour = draw_neighbour(jax.random.fold_in(splits[6], 71), part)
    return dict(traces=traces, operator=operator, freq_bins=freq_bins, win_lengths=win_lengths, coefficients=coefficients, neighbour=neighbour)


def angle_grid(freq_bins):
    sample_index = jnp.arange(NT, dtype=jnp.int32)
    phases = (sample_index[:, None] * freq_bins[None, :]) % NT
    return (2.0 * math.pi / NT) * phases.astype(jnp.float32)


def matching(multiple_estimate, coefficients, win_lengths):
    half_taps = (TAPS - 1) // 2
    window_ends = jnp.cumsum(win_lengths)
    sample_index = jnp.arange(NT, dtype=jnp.int32)
    window = jnp.sum((window_ends[None, :] <= sample_index[:, None]).astype(jnp.int32), axis=1)
    membership = (window[:, None] == jnp.arange(NWIN, dtype=jnp.int32)[None, :]).astype(jnp.float32)
    per_sample = jnp.dot(membership, coefficients, precision=lax.Precision.HIGHEST)
    padded = jnp.pad(multiple_estimate, ((0, 0), (0, 0), (half_taps, half_taps)))
    summed = jnp.zeros_like(multiple_estimate)
    for lag_index in range(TAPS):
        summed = summed + per_sample[:, lag_index] * padded[:, :, lag_index:lag_index + NT]
    return summed


def reference(traces, operator, freq_bins, win_lengths, coefficients, neighbour):
    angles = angle_grid(freq_bins)
    forward = jnp.stack([jnp.cos(angles), -jnp.sin(angles)], axis=2).reshape(NT, 2 * F).astype(jnp.bfloat16)
    spectra = jnp.dot(traces.reshape(NPTS * SHOTS, NT), forward, preferred_element_type=jnp.float32).astype(jnp.bfloat16)
    spectra = spectra.reshape(NPTS, SHOTS, F, 2).transpose(0, 2, 3, 1)
    dims = (((0,), (0,)), ((), ()))
    frequency_slices = []
    for freq_index in range(F):
        op_real = operator[:, freq_index, 0, :]
        op_imag = operator[:, freq_index, 1, :]
        sp_real = spectra[:, freq_index, 0, :]
        spectrum_imaginary = spectra[:, freq_index, 1, :]
        real_part = lax.dot_general(op_real, sp_real, dims, preferred_element_type=jnp.float32) - lax.dot_general(op_imag, spectrum_imaginary, dims, preferred_element_type=jnp.float32)
        imag_part = lax.dot_general(op_real, spectrum_imaginary, dims, preferred_element_type=jnp.float32) + lax.dot_general(op_imag, sp_real, dims, preferred_element_type=jnp.float32)
        frequency_slices.append(jnp.stack([real_part, imag_part], axis=1))
    predicted_multiples = jnp.stack(frequency_slices, axis=1)
    norm_divisor = (2.0 * F * NT) ** -0.5
    inverse_transform = norm_divisor * jnp.stack([jnp.cos(angles.T), -jnp.sin(angles.T)], axis=1)
    multiple_estimate = jnp.einsum("izwj,zwn->ijn", predicted_multiples, inverse_transform, precision=lax.Precision.HIGHEST)
    blocks = multiple_estimate.reshape(NPTS // 256, 256, SHOTS, NT)
    filtered = lax.map(lambda span_rows: matching(span_rows, coefficients, win_lengths), blocks).reshape(NPTS, SHOTS, NT)
    padded = jnp.pad(filtered, ((HALO, HALO), (0, 0), (0, 0)))
    adapted = filtered
    for offset in range(-HALO, HALO + 1):
        selector = (neighbour == offset).astype(jnp.float32)[:, None, None]
        adapted = adapted + 0.5 * selector * padded[HALO + offset:HALO + offset + NPTS]
    return (traces.astype(jnp.float32) - adapted).astype(jnp.bfloat16)
```

```python
import functools
import math

import jax
import jax.numpy as jnp
from jax import lax
from jax.experimental import pallas as pl
from jax.experimental.pallas import tpu as pltpu
from jax.sharding import PartitionSpec as P

TAPS = 31
HALO = 2
VMEM_LIMIT = 60 * 1024 * 1024
NT_DIMS = (((1,), (1,)), ((), ()))
TN_DIMS = (((0,), (0,)), ((), ()))


def angle_grid(freq_bins, samples):
    sample_index = jnp.arange(samples, dtype=jnp.int32)
    phases = sample_index[:, None] * freq_bins[None, :] % samples
    return 2.0 * math.pi / samples * phases.astype(jnp.float32)


def matching(multiple_estimate, coefficients, win_lengths):
    samples = multiple_estimate.shape[1]
    half_taps = (TAPS - 1) // 2
    order = jnp.arange(win_lengths.shape[0], dtype=jnp.int32)
    window_ends = jnp.sum(jnp.where(order[:, None] <= order[None, :], win_lengths[:, None], 0), axis=0)
    sample_index = jnp.arange(samples, dtype=jnp.int32)
    window = jnp.sum((window_ends[None, :] <= sample_index[:, None]).astype(jnp.int32), axis=1)
    membership = (
        window[None, :] == jnp.arange(coefficients.shape[0], dtype=jnp.int32)[:, None]
    ).astype(jnp.float32)
    per_sample = jnp.dot(coefficients.T, membership, precision=lax.Precision.HIGHEST)
    padded = jnp.pad(multiple_estimate, ((0, 0), (half_taps, half_taps)))
    summed = jnp.zeros_like(multiple_estimate)
    for lag_index in range(TAPS):
        summed = summed + per_sample[lag_index][None] * padded[:, lag_index : lag_index + samples]
    return summed


def swap_halves(x, half):
    return pltpu.roll(x, half, axis=1)


def forward_kernel(freq_count, shots, traces_ref, table_ref, out_ref, lines):
    points = out_ref.shape[1]
    lanes = 2 * shots
    spectra = lax.dot_general(
        table_ref[...], traces_ref[...], NT_DIMS, preferred_element_type=jnp.float32
    )
    low = lax.broadcasted_iota(jnp.int32, (freq_count, lanes), 1) < shots
    for pair in range(points // 2):
        cols = slice(pair * lanes, (pair + 1) * lanes)
        real, imag = spectra[:freq_count, cols], spectra[freq_count:, cols]
        first = jnp.where(low, real, swap_halves(imag, shots))
        second = jnp.where(low, swap_halves(real, shots), imag)
        at = 2 * pair * freq_count
        lines[at : at + freq_count, :] = first
        lines[at + freq_count : at + 2 * freq_count, :] = second
    for f in range(freq_count):
        out_ref[f] = lines[pl.ds(f, points, stride=freq_count), :].astype(out_ref.dtype)


def forward(traces2, table, freq_count, shots, points, chunk, chunks):
    rows, samples = traces2.shape
    rows = rows // chunks
    local = rows // shots
    first = chunk * (local // points)
    return pl.pallas_call(
        functools.partial(forward_kernel, freq_count, shots),
        out_shape=jax.ShapeDtypeStruct((freq_count, local, 2 * shots), jnp.bfloat16),
        grid=(local // points,),
        in_specs=[
            pl.BlockSpec((points * shots, samples), lambda i: (first + i, 0)),
            pl.BlockSpec((2 * freq_count, samples), lambda i: (0, 0)),
        ],
        out_specs=pl.BlockSpec((freq_count, points, 2 * shots), lambda i: (0, i, 0)),
        scratch_shapes=[pltpu.VMEM((points * freq_count, 2 * shots), jnp.float32)],
        compiler_params=pltpu.CompilerParams(
            vmem_limit_bytes=VMEM_LIMIT, dimension_semantics=("arbitrary",)
        ),
        cost_estimate=pl.CostEstimate(
            flops=4 * freq_count * rows * samples,
            bytes_accessed=2 * rows * samples,
            transcendentals=0,
        ),
    )(traces2, table)


def combined(real_rows, imag_rows, shots):
    low = lax.broadcasted_iota(jnp.int32, real_rows.shape, 1) < shots
    return real_rows + jnp.where(low, -1.0, 1.0) * swap_halves(imag_rows, shots)


def products(operator_refs, edge_refs, spectra_ref, shots):
    spectra = spectra_ref[:, 0].reshape(-1, 2 * shots)
    planes = [
        jnp.concatenate([ref[0, part] for ref in operator_refs], axis=1) for part in range(2)
    ]
    planes.append(jnp.concatenate([ref[0] for ref in edge_refs], axis=1))
    real, imag, edge = [
        jnp.dot(plane, spectra, preferred_element_type=jnp.float32) for plane in planes
    ]
    return combined(real, imag, shots), combined(edge[0:8], edge[8:16], shots)


def partial_kernel(shots, pieces, *refs):
    operator_refs, edge_refs = refs[:pieces], refs[pieces : 2 * pieces]
    spectra_ref, out_ref = refs[2 * pieces :]
    local = operator_refs[0].shape[2]
    main, edge = products(operator_refs, edge_refs, spectra_ref, shots)
    out_ref[0, 8 : 8 + local, :] = main
    out_ref[0, 0:8, :] = edge


def source_specs(local, sources, parts, chunk, chunks, f_of):
    pieces = parts if chunks > 1 else 1
    width = sources // (pieces * chunks)

    def column(piece):
        return piece * chunks + chunk

    operator_specs = [
        pl.BlockSpec((1, 2, local, width), lambda i, c=column(p): (f_of(i), 0, 0, c))
        for p in range(pieces)
    ]
    edge_specs = [
        pl.BlockSpec((1, 16, width), lambda i, c=column(p): (f_of(i), 0, c))
        for p in range(pieces)
    ]
    return pieces, operator_specs, edge_specs


def partial_product(operator, edge, spectra, shots, chunk, chunks):
    freq_count, _, local, sources = operator.shape
    parts, _, mine, lanes = spectra.shape
    pieces, operator_specs, edge_specs = source_specs(
        local, sources, parts, chunk, chunks, lambda i: i
    )
    return pl.pallas_call(
        functools.partial(partial_kernel, shots, pieces),
        out_shape=jax.ShapeDtypeStruct((freq_count, local + 8, lanes), jnp.float32),
        grid=(freq_count,),
        in_specs=operator_specs
        + edge_specs
        + [pl.BlockSpec((parts, 1, mine, lanes), lambda i: (0, i, 0, 0))],
        out_specs=pl.BlockSpec((1, local + 8, lanes), lambda i: (i, 0, 0)),
        compiler_params=pltpu.CompilerParams(
            vmem_limit_bytes=VMEM_LIMIT, dimension_semantics=("arbitrary",)
        ),
        cost_estimate=pl.CostEstimate(
            flops=4 * freq_count * local * (sources // chunks) * lanes,
            bytes_accessed=4 * freq_count * local * (sources // chunks),
            transcendentals=0,
        ),
    )(*([operator] * pieces), *([edge] * pieces), spectra)


def adapt_kernel(freq_count, shots, points, pieces, partials, *refs):
    near_ref, operator_refs, edge_refs = refs[0], refs[1 : 1 + pieces], refs[1 + pieces : 1 + 2 * pieces]
    spectra_ref = refs[1 + 2 * pieces]
    partial_refs = refs[2 + 2 * pieces : 2 + 2 * pieces + partials]
    basis_ref, traces_ref, out_ref, predicted, lines, split_basis = refs[2 + 2 * pieces + partials :]
    step = pl.program_id(0)
    local = operator_refs[0].shape[2]
    lanes = 2 * shots
    terms = 2 * freq_count

    @pl.when(step == 0)
    def _():
        basis = basis_ref[...]
        high = basis.astype(jnp.bfloat16)
        split_basis[0:terms, :] = high
        split_basis[terms : 2 * terms, :] = high
        split_basis[2 * terms :, :] = (basis - high.astype(jnp.float32)).astype(jnp.bfloat16)

    @pl.when(step < freq_count)
    def _():
        main, edge = products(operator_refs, edge_refs, spectra_ref, shots)
        for ref in partial_refs:
            main = main + ref[0, 8 : 8 + local, :]
            edge = edge + ref[0, 0:8, :]
        predicted[step, 8 : 8 + local, :] = main
        predicted[step, 0:8, :] = edge

    @pl.when(step == freq_count - 1)
    def _():
        for f in range(freq_count):
            mine = predicted[f, 8 : 8 + local, :]
            lines[pl.ds(HALO * freq_count + f, local, stride=freq_count), :] = mine
            for h in range(HALO):
                before = h * freq_count + f
                lines[before : before + 1, :] = predicted[f, h : h + 1, :]
                after = (HALO + local + h) * freq_count + f
                lines[after : after + 1, :] = predicted[f, HALO + h : HALO + h + 1, :]

    @pl.when(step >= freq_count)
    def _():
        start = (step - freq_count) * points
        low = lax.broadcasted_iota(jnp.int32, (freq_count, lanes), 1) < shots

        def mixed(point):
            own = pl.multiple_of((point + HALO) * freq_count, freq_count)
            other = pl.multiple_of((point + HALO + near_ref[point]) * freq_count, freq_count)
            return lines[pl.ds(own, freq_count), :] + 0.5 * lines[pl.ds(other, freq_count), :]

        group = 8
        for part in range(points // group):
            reals, imags = [], []
            for pair in range(group // 2):
                first = mixed(start + part * group + 2 * pair)
                second = mixed(start + part * group + 2 * pair + 1)
                reals.append(jnp.where(low, first, swap_halves(second, shots)))
                imags.append(jnp.where(low, swap_halves(first, shots), second))
            terms_by_row = jnp.concatenate(
                [jnp.concatenate(reals, axis=1), jnp.concatenate(imags, axis=1)], axis=0
            )
            high = terms_by_row.astype(jnp.bfloat16)
            rest = (terms_by_row - high.astype(jnp.float32)).astype(jnp.bfloat16)
            left = jnp.concatenate([high, rest, high], axis=0)
            adapted = lax.dot_general(
                left, split_basis[...], TN_DIMS, preferred_element_type=jnp.float32
            )
            rows = slice(part * group * shots, (part + 1) * group * shots)
            out_ref[rows, :] = (traces_ref[rows, :].astype(jnp.float32) - adapted).astype(
                out_ref.dtype
            )


def adapt(near, operator, edge, spectra, partial, basis, traces2, shots, points, chunk, chunks):
    freq_count, _, local, sources = operator.shape
    rows, samples = traces2.shape
    parts, _, mine, lanes = spectra.shape
    block = points * shots

    def f_of(i):
        return jnp.minimum(i, freq_count - 1)

    def row_of(i):
        return jnp.maximum(i - freq_count, 0)

    pieces, operator_specs, edge_specs = source_specs(local, sources, parts, chunk, chunks, f_of)
    partial_specs = [
        pl.BlockSpec((1, local + 8, lanes), lambda i: (f_of(i), 0, 0)) for _ in partial
    ]
    return pl.pallas_call(
        functools.partial(adapt_kernel, freq_count, shots, points, pieces, len(partial)),
        out_shape=jax.ShapeDtypeStruct((rows, samples), jnp.bfloat16),
        grid=(freq_count + local // points,),
        in_specs=[pl.BlockSpec(memory_space=pltpu.SMEM)]
        + operator_specs
        + edge_specs
        + [pl.BlockSpec((parts, 1, mine, lanes), lambda i: (0, f_of(i), 0, 0))]
        + partial_specs
        + [
            pl.BlockSpec((2 * freq_count, samples), lambda i: (0, 0)),
            pl.BlockSpec((block, samples), lambda i: (row_of(i), 0)),
        ],
        out_specs=pl.BlockSpec((block, samples), lambda i: (row_of(i), 0)),
        scratch_shapes=[
            pltpu.VMEM((freq_count, local + 8, lanes), jnp.float32),
            pltpu.VMEM(((local + 2 * HALO) * freq_count, lanes), jnp.float32),
            pltpu.VMEM((6 * freq_count, samples), jnp.bfloat16),
        ],
        compiler_params=pltpu.CompilerParams(
            vmem_limit_bytes=VMEM_LIMIT, dimension_semantics=("arbitrary",)
        ),
    )(near, *([operator] * pieces), *([edge] * pieces), spectra, *partial, basis, traces2)


def on_device(traces, operator, freq_bins, win_lengths, coefficients, neighbour):
    local, shots, samples = traces.shape
    freq_count = freq_bins.shape[0]
    size = lax.axis_size("surf")
    points = 32
    up = [(i, i + 1) for i in range(size - 1)]
    down = [(j, i) for i, j in up]
    before = lax.ppermute(operator[local - HALO :], "surf", up)
    after = lax.ppermute(operator[:HALO], "surf", down)
    edge = jnp.concatenate([before, after], axis=0).transpose(1, 2, 0, 3)
    edge = jnp.pad(edge, ((0, 0), (0, 0), (0, 8 - 2 * HALO), (0, 0)))
    edge = edge.reshape(freq_count, 16, operator.shape[3])

    angles = angle_grid(freq_bins, samples)
    table = jnp.concatenate([jnp.cos(angles.T), -jnp.sin(angles.T)], axis=0)
    norm = (2.0 * freq_count * samples) ** (-0.5)
    basis = matching(norm * table, coefficients, win_lengths)

    traces2 = traces.reshape(local * shots, samples)
    bf16_table = table.astype(jnp.bfloat16)
    chunks = 1
    gathered = []
    for chunk in range(chunks):
        spectra = forward(traces2, bf16_table, freq_count, shots, points, chunk, chunks)
        gathered.append(lax.all_gather(spectra, "surf"))
    by_freq = operator.transpose(1, 2, 0, 3)
    partial = []
    for chunk in range(chunks - 1):
        partial.append(partial_product(by_freq, edge, gathered[chunk], shots, chunk, chunks))
    out = adapt(
        neighbour, by_freq, edge, gathered[-1], partial, basis, traces2,
        shots, points, chunks - 1, chunks,
    )
    return out.reshape(local, shots, samples)


def solution(mesh):
    return jax.shard_map(
        on_device,
        mesh=mesh,
        in_specs=(P("surf", "group", None), P("surf", None, None, None), P(), P(), P(), P("surf")),
        out_specs=P("surf", "group", None),
        check_vma=False,
    )
```

```python
import functools
import math

import jax
import jax.numpy as jnp
from jax import lax
from jax.experimental import pallas as pl
from jax.experimental.pallas import tpu as pltpu
from jax.sharding import PartitionSpec as P

TAPS = 31
HALO = 2
VMEM_LIMIT = 60 * 1024 * 1024
NT_DIMS = (((1,), (1,)), ((), ()))
TN_DIMS = (((0,), (0,)), ((), ()))


def angle_grid(freq_bins, samples):
    sample_index = jnp.arange(samples, dtype=jnp.int32)
    phases = sample_index[:, None] * freq_bins[None, :] % samples
    return 2.0 * math.pi / samples * phases.astype(jnp.float32)


def matching(multiple_estimate, coefficients, win_lengths):
    samples = multiple_estimate.shape[1]
    half_taps = (TAPS - 1) // 2
    order = jnp.arange(win_lengths.shape[0], dtype=jnp.int32)
    window_ends = jnp.sum(jnp.where(order[:, None] <= order[None, :], win_lengths[:, None], 0), axis=0)
    sample_index = jnp.arange(samples, dtype=jnp.int32)
    window = jnp.sum((window_ends[None, :] <= sample_index[:, None]).astype(jnp.int32), axis=1)
    membership = (
        window[None, :] == jnp.arange(coefficients.shape[0], dtype=jnp.int32)[:, None]
    ).astype(jnp.float32)
    per_sample = jnp.dot(coefficients.T, membership, precision=lax.Precision.HIGHEST)
    padded = jnp.pad(multiple_estimate, ((0, 0), (half_taps, half_taps)))
    summed = jnp.zeros_like(multiple_estimate)
    for lag_index in range(TAPS):
        summed = summed + per_sample[lag_index][None] * padded[:, lag_index : lag_index + samples]
    return summed


def swap_halves(x, half):
    return pltpu.roll(x, half, axis=1)


def forward_kernel(freq_count, shots, traces_ref, table_ref, out_ref, lines):
    points = out_ref.shape[1]
    lanes = 2 * shots
    spectra = lax.dot_general(
        table_ref[...], traces_ref[...], NT_DIMS, preferred_element_type=jnp.float32
    )
    low = lax.broadcasted_iota(jnp.int32, (freq_count, lanes), 1) < shots
    for pair in range(points // 2):
        cols = slice(pair * lanes, (pair + 1) * lanes)
        real, imag = spectra[:freq_count, cols], spectra[freq_count:, cols]
        first = jnp.where(low, real, swap_halves(imag, shots))
        second = jnp.where(low, swap_halves(real, shots), imag)
        at = 2 * pair * freq_count
        lines[at : at + freq_count, :] = first
        lines[at + freq_count : at + 2 * freq_count, :] = second
    for f in range(freq_count):
        out_ref[f] = lines[pl.ds(f, points, stride=freq_count), :].astype(out_ref.dtype)


def forward(traces2, table, freq_count, shots, points, chunk, chunks):
    rows, samples = traces2.shape
    rows = rows // chunks
    local = rows // shots
    first = chunk * (local // points)
    return pl.pallas_call(
        functools.partial(forward_kernel, freq_count, shots),
        out_shape=jax.ShapeDtypeStruct((freq_count, local, 2 * shots), jnp.bfloat16),
        grid=(local // points,),
        in_specs=[
            pl.BlockSpec((points * shots, samples), lambda i: (first + i, 0)),
            pl.BlockSpec((2 * freq_count, samples), lambda i: (0, 0)),
        ],
        out_specs=pl.BlockSpec((freq_count, points, 2 * shots), lambda i: (0, i, 0)),
        scratch_shapes=[pltpu.VMEM((points * freq_count, 2 * shots), jnp.float32)],
        compiler_params=pltpu.CompilerParams(
            vmem_limit_bytes=VMEM_LIMIT, dimension_semantics=("arbitrary",)
        ),
        cost_estimate=pl.CostEstimate(
            flops=4 * freq_count * rows * samples,
            bytes_accessed=2 * rows * samples,
            transcendentals=0,
        ),
    )(traces2, table)


def combined(real_rows, imag_rows, shots):
    low = lax.broadcasted_iota(jnp.int32, real_rows.shape, 1) < shots
    return real_rows + jnp.where(low, -1.0, 1.0) * swap_halves(imag_rows, shots)


def products(operator_refs, edge_refs, spectra_ref, shots):
    spectra = spectra_ref[:, 0].reshape(-1, 2 * shots)
    planes = [
        jnp.concatenate([ref[0, part] for ref in operator_refs], axis=1) for part in range(2)
    ]
    planes.append(jnp.concatenate([ref[0] for ref in edge_refs], axis=1))
    real, imag, edge = [
        jnp.dot(plane, spectra, preferred_element_type=jnp.float32) for plane in planes
    ]
    return combined(real, imag, shots), combined(edge[0:8], edge[8:16], shots)


def partial_kernel(shots, pieces, *refs):
    operator_refs, edge_refs = refs[:pieces], refs[pieces : 2 * pieces]
    spectra_ref, out_ref = refs[2 * pieces :]
    local = operator_refs[0].shape[2]
    main, edge = products(operator_refs, edge_refs, spectra_ref, shots)
    out_ref[0, 8 : 8 + local, :] = main
    out_ref[0, 0:8, :] = edge


def source_specs(local, sources, parts, chunk, chunks, f_of):
    pieces = parts if chunks > 1 else 1
    width = sources // (pieces * chunks)

    def column(piece):
        return piece * chunks + chunk

    operator_specs = [
        pl.BlockSpec((1, 2, local, width), lambda i, c=column(p): (f_of(i), 0, 0, c))
        for p in range(pieces)
    ]
    edge_specs = [
        pl.BlockSpec((1, 16, width), lambda i, c=column(p): (f_of(i), 0, c))
        for p in range(pieces)
    ]
    return pieces, operator_specs, edge_specs


def partial_product(operator, edge, spectra, shots, chunk, chunks):
    freq_count, _, local, sources = operator.shape
    parts, _, mine, lanes = spectra.shape
    pieces, operator_specs, edge_specs = source_specs(
        local, sources, parts, chunk, chunks, lambda i: i
    )
    return pl.pallas_call(
        functools.partial(partial_kernel, shots, pieces),
        out_shape=jax.ShapeDtypeStruct((freq_count, local + 8, lanes), jnp.float32),
        grid=(freq_count,),
        in_specs=operator_specs
        + edge_specs
        + [pl.BlockSpec((parts, 1, mine, lanes), lambda i: (0, i, 0, 0))],
        out_specs=pl.BlockSpec((1, local + 8, lanes), lambda i: (i, 0, 0)),
        compiler_params=pltpu.CompilerParams(
            vmem_limit_bytes=VMEM_LIMIT, dimension_semantics=("arbitrary",)
        ),
        cost_estimate=pl.CostEstimate(
            flops=4 * freq_count * local * (sources // chunks) * lanes,
            bytes_accessed=4 * freq_count * local * (sources // chunks),
            transcendentals=0,
        ),
    )(*([operator] * pieces), *([edge] * pieces), spectra)


def adapt_kernel(freq_count, shots, points, pieces, partials, *refs):
    near_ref, operator_refs, edge_refs = refs[0], refs[1 : 1 + pieces], refs[1 + pieces : 1 + 2 * pieces]
    spectra_ref = refs[1 + 2 * pieces]
    partial_refs = refs[2 + 2 * pieces : 2 + 2 * pieces + partials]
    basis_ref, traces_ref, out_ref, predicted, lines, split_basis = refs[2 + 2 * pieces + partials :]
    step = pl.program_id(0)
    local = operator_refs[0].shape[2]
    lanes = 2 * shots
    terms = 2 * freq_count

    @pl.when(step == 0)
    def _():
        basis = basis_ref[...]
        high = basis.astype(jnp.bfloat16)
        split_basis[0:terms, :] = high
        split_basis[terms : 2 * terms, :] = high
        split_basis[2 * terms :, :] = (basis - high.astype(jnp.float32)).astype(jnp.bfloat16)

    @pl.when(step < freq_count)
    def _():
        main, edge = products(operator_refs, edge_refs, spectra_ref, shots)
        for ref in partial_refs:
            main = main + ref[0, 8 : 8 + local, :]
            edge = edge + ref[0, 0:8, :]
        predicted[step, 8 : 8 + local, :] = main
        predicted[step, 0:8, :] = edge

    @pl.when(step == freq_count - 1)
    def _():
        for f in range(freq_count):
            mine = predicted[f, 8 : 8 + local, :]
            lines[pl.ds(HALO * freq_count + f, local, stride=freq_count), :] = mine
            for h in range(HALO):
                before = h * freq_count + f
                lines[before : before + 1, :] = predicted[f, h : h + 1, :]
                after = (HALO + local + h) * freq_count + f
                lines[after : after + 1, :] = predicted[f, HALO + h : HALO + h + 1, :]

    @pl.when(step >= freq_count)
    def _():
        start = (step - freq_count) * points
        low = lax.broadcasted_iota(jnp.int32, (freq_count, lanes), 1) < shots

        def mixed(point):
            own = pl.multiple_of((point + HALO) * freq_count, freq_count)
            other = pl.multiple_of((point + HALO + near_ref[point]) * freq_count, freq_count)
            return lines[pl.ds(own, freq_count), :] + 0.5 * lines[pl.ds(other, freq_count), :]

        group = 8
        for part in range(points // group):
            reals, imags = [], []
            for pair in range(group // 2):
                first = mixed(start + part * group + 2 * pair)
                second = mixed(start + part * group + 2 * pair + 1)
                reals.append(jnp.where(low, first, swap_halves(second, shots)))
                imags.append(jnp.where(low, swap_halves(first, shots), second))
            terms_by_row = jnp.concatenate(
                [jnp.concatenate(reals, axis=1), jnp.concatenate(imags, axis=1)], axis=0
            )
            high = terms_by_row.astype(jnp.bfloat16)
            rest = (terms_by_row - high.astype(jnp.float32)).astype(jnp.bfloat16)
            left = jnp.concatenate([high, rest, high], axis=0)
            adapted = lax.dot_general(
                left, split_basis[...], TN_DIMS, preferred_element_type=jnp.float32
            )
            rows = slice(part * group * shots, (part + 1) * group * shots)
            out_ref[rows, :] = (traces_ref[rows, :].astype(jnp.float32) - adapted).astype(
                out_ref.dtype
            )


def adapt(near, operator, edge, spectra, partial, basis, traces2, shots, points, chunk, chunks):
    freq_count, _, local, sources = operator.shape
    rows, samples = traces2.shape
    parts, _, mine, lanes = spectra.shape
    block = points * shots

    def f_of(i):
        return jnp.minimum(i, freq_count - 1)

    def row_of(i):
        return jnp.maximum(i - freq_count, 0)

    pieces, operator_specs, edge_specs = source_specs(local, sources, parts, chunk, chunks, f_of)
    partial_specs = [
        pl.BlockSpec((1, local + 8, lanes), lambda i: (f_of(i), 0, 0)) for _ in partial
    ]
    return pl.pallas_call(
        functools.partial(adapt_kernel, freq_count, shots, points, pieces, len(partial)),
        out_shape=jax.ShapeDtypeStruct((rows, samples), jnp.bfloat16),
        grid=(freq_count + local // points,),
        in_specs=[pl.BlockSpec(memory_space=pltpu.SMEM)]
        + operator_specs
        + edge_specs
        + [pl.BlockSpec((parts, 1, mine, lanes), lambda i: (0, f_of(i), 0, 0))]
        + partial_specs
        + [
            pl.BlockSpec((2 * freq_count, samples), lambda i: (0, 0)),
            pl.BlockSpec((block, samples), lambda i: (row_of(i), 0)),
        ],
        out_specs=pl.BlockSpec((block, samples), lambda i: (row_of(i), 0)),
        scratch_shapes=[
            pltpu.VMEM((freq_count, local + 8, lanes), jnp.float32),
            pltpu.VMEM(((local + 2 * HALO) * freq_count, lanes), jnp.float32),
            pltpu.VMEM((6 * freq_count, samples), jnp.bfloat16),
        ],
        compiler_params=pltpu.CompilerParams(
            vmem_limit_bytes=VMEM_LIMIT, dimension_semantics=("arbitrary",)
        ),
    )(near, *([operator] * pieces), *([edge] * pieces), spectra, *partial, basis, traces2)


MESH = pl.DeviceIdType.MESH
BF16_LANES = 128


def place(size):
    me = lax.axis_index("surf")
    chips = size // 2
    chip, core = me // 2, me % 2
    position = jnp.where(chip % 2 == 0, chip // 2, chips - 1 - chip // 2)
    return me, core, position, 1 - 2 * core


def device_at(position, core, chips):
    position = (position + chips) % chips
    chip = jnp.where(position < chips // 2, 2 * position, 2 * (chips - 1 - position) + 1)
    return 2 * chip + core


def predict_kernel(
    size, freq_count, shots, local, points, subs, *refs
):
    traces, table, operator, lines = refs[:4]
    held, held_sem, planes, planes_sem, spectra, total, rows = refs[4:11]
    edge_out, edge_in = refs[11:13]
    ring_send, ring_recv, pair_send, pair_recv, edge_send, edge_recv = refs[13:]
    chips = size // 2
    lanes = 2 * shots
    me, core, position, toward = place(size)
    pair = me + 1 - 2 * core
    after = device_at(position + toward, core, chips)
    before = device_at(position - toward, core, chips)
    beside = (me + 2 * core - 1 + size) % size
    tiles = local // BF16_LANES
    chunks = local // points
    sub_points = local // subs
    per_sub = chunks // subs
    slots = held.shape[0]
    block_rows = points * shots

    def origin(step, which):
        sign = toward * (1 - 2 * which)
        return device_at(position - step * sign, core + which - 2 * core * which, chips)

    def held_copy(chunk):
        slot = chunk % slots
        return pltpu.make_async_copy(
            traces.at[pl.ds(pl.multiple_of(chunk * block_rows, block_rows), block_rows)],
            held.at[slot],
            held_sem.at[slot],
        )

    def fetch_planes(order):
        dev = origin(order // 2, order % 2)

        def one(f, carry):
            for tile in range(tiles):
                at = dev * tiles + tile
                pltpu.make_async_copy(
                    operator.at[:, f, at], planes.at[f, at], planes_sem.at[order]
                ).start()
            return carry

        lax.fori_loop(0, freq_count, one, 0)

    def part(dev, sub):
        return spectra.at[dev, :, pl.ds(pl.multiple_of(sub * sub_points, sub_points), sub_points), :]

    def ring_copy(step, sub):
        ref = part(origin(step, 0), sub)
        return pltpu.make_async_remote_copy(
            ref, ref, ring_send.at[step, sub], ring_recv.at[step + 1, sub],
            device_id={"surf": after}, device_id_type=MESH,
        )

    def pair_copy(step, sub):
        ref = part(origin(step, 0), sub)
        return pltpu.make_async_remote_copy(
            ref, ref, pair_send.at[step, sub], pair_recv.at[step, sub],
            device_id={"surf": pair}, device_id_type=MESH,
        )

    def arrive(step, sub):
        ref = part(origin(step, 0), sub)
        pltpu.make_async_remote_copy(
            ref, ref, ring_send.at[step - 1, sub], ring_recv.at[step, sub],
            device_id={"surf": after}, device_id_type=MESH,
        ).wait_recv()

    def arrive_pair(step, sub):
        ref = part(origin(step, 1), sub)
        pltpu.make_async_remote_copy(
            ref, ref, pair_send.at[step, sub], pair_recv.at[step, sub],
            device_id={"surf": pair}, device_id_type=MESH,
        ).wait_recv()

    def product(order):
        dev = origin(order // 2, order % 2)
        block = planes.at[:, pl.ds(dev * tiles, tiles)]
        pltpu.make_async_copy(block, block, planes_sem.at[order]).wait()
        flat = planes.reshape(freq_count, size * tiles, 2 * local, BF16_LANES)
        for f in range(freq_count):
            left = jnp.concatenate([flat[f, dev * tiles + tile] for tile in range(tiles)], axis=1)
            total[f] += jnp.dot(left, spectra[dev, f], preferred_element_type=jnp.float32)

    for chunk in range(slots - 1):
        held_copy(chunk).start()

    barrier = pltpu.get_barrier_semaphore()
    for other in (after, before, pair, beside):
        pl.semaphore_signal(barrier, inc=1, device_id={"surf": other}, device_id_type=MESH)
    total[...] = jnp.zeros_like(total)
    pl.semaphore_wait(barrier, 4)

    low = lax.broadcasted_iota(jnp.int32, (freq_count, lanes), 1) < shots

    def forward(chunk, carry):
        @pl.when(chunk + slots - 1 < chunks)
        def _():
            held_copy(chunk + slots - 1).start()

        for order in range(size // chunks):
            fetch_planes(chunk * (size // chunks) + order)
        held_copy(chunk).wait()
        found = lax.dot_general(
            table[...], held[chunk % slots], NT_DIMS, preferred_element_type=jnp.float32
        )
        for two in range(points // 2):
            cols = slice(two * lanes, (two + 1) * lanes)
            real, imag = found[:freq_count, cols], found[freq_count:, cols]
            first = jnp.where(low, real, swap_halves(imag, shots))
            second = jnp.where(low, swap_halves(real, shots), imag)
            at = 2 * two * freq_count
            rows[at : at + freq_count, :] = first
            rows[at + freq_count : at + 2 * freq_count, :] = second
        start = pl.multiple_of(chunk * points, points)
        for f in range(freq_count):
            spectra[me, f, pl.ds(start, points), :] = rows[
                pl.ds(f, points, stride=freq_count), :
            ].astype(spectra.dtype)
        return carry

    for sub in range(subs):
        lax.fori_loop(sub * per_sub, (sub + 1) * per_sub, forward, 0)
        for older in range(sub, -1, -1):
            step = sub - older
            if step <= chips - 1:
                if step > 0:
                    arrive(step, older)
                if step < chips - 1:
                    ring_copy(step, older).start()
                pair_copy(step, older).start()

    def both(step):
        product(2 * step)
        for sub in range(subs):
            arrive_pair(step, sub)
        product(2 * step + 1)

    def onward(front, carry):
        both(front - subs)
        for sub in range(subs - 1, -1, -1):
            step = front - sub

            @pl.when(step <= chips - 1)
            def _():
                arrive(step, sub)

                @pl.when(step < chips - 1)
                def _():
                    ring_copy(step, sub).start()

                pair_copy(step, sub).start()

        return carry

    lax.fori_loop(subs, chips + subs - 1, onward, 0)
    both(chips - 1)

    low_all = lax.broadcasted_iota(jnp.int32, (local, lanes), 1) < shots
    sign = jnp.where(low_all, -1.0, 1.0)
    for f in range(freq_count):
        real = total[f, pl.ds(0, local, stride=2), :]
        imag = total[f, pl.ds(1, local, stride=2), :]
        lines[pl.ds(HALO * freq_count + f, local, stride=freq_count), :] = (
            real + sign * swap_halves(imag, shots)
        )
    width = HALO * freq_count
    edge_out[0] = lines[width : 2 * width, :]
    edge_out[1] = lines[local * freq_count : local * freq_count + width, :]

    def edge_copy(which, to):
        return pltpu.make_async_remote_copy(
            edge_out.at[which], edge_in.at[1 - which], edge_send.at[which], edge_recv.at[1 - which],
            device_id={"surf": to}, device_id_type=MESH,
        )

    previous, following = (me + size - 1) % size, (me + 1) % size
    edges = [edge_copy(0, previous), edge_copy(1, following)]
    for copy in edges:
        copy.start()
    for copy in edges:
        copy.wait()
    lines[0:width, :] = jnp.where(me > 0, edge_in[0], 0.0)
    lines[width + local * freq_count :, :] = jnp.where(me < size - 1, edge_in[1], 0.0)

    def drain(step, carry):
        for sub in range(subs):
            @pl.when(step < chips - 1)
            def _():
                ring_copy(step, sub).wait_send()

            pair_copy(step, sub).wait_send()
        return carry

    lax.fori_loop(0, chips, drain, 0)


def predict(traces2, table, operator, freq_count, shots, local, size, points, subs):
    rows, samples = traces2.shape
    sources = operator.shape[3]
    lanes = 2 * shots
    tiles = sources // BF16_LANES
    tiled = operator.reshape(local, freq_count, 2, tiles, BF16_LANES).transpose(0, 1, 3, 2, 4)
    chips = size // 2
    slots = 3
    width = HALO * freq_count
    return pl.pallas_call(
        functools.partial(predict_kernel, size, freq_count, shots, local, points, subs),
        out_shape=jax.ShapeDtypeStruct(((local + 2 * HALO) * freq_count, lanes), jnp.float32),
        in_specs=[
            pl.BlockSpec(memory_space=pl.ANY),
            pl.BlockSpec(memory_space=pltpu.VMEM),
            pl.BlockSpec(memory_space=pl.ANY),
        ],
        out_specs=pl.BlockSpec(memory_space=pltpu.VMEM),
        scratch_shapes=[
            pltpu.VMEM((slots, points * shots, samples), jnp.bfloat16),
            pltpu.SemaphoreType.DMA((slots,)),
            pltpu.VMEM((freq_count, tiles, local, 2, BF16_LANES), jnp.bfloat16),
            pltpu.SemaphoreType.DMA((size,)),
            pltpu.VMEM((size, freq_count, local, lanes), jnp.bfloat16),
            pltpu.VMEM((freq_count, 2 * local, lanes), jnp.float32),
            pltpu.VMEM((points * freq_count, lanes), jnp.float32),
            pltpu.VMEM((2, width, lanes), jnp.float32),
            pltpu.VMEM((2, width, lanes), jnp.float32),
            pltpu.SemaphoreType.DMA((chips, subs)),
            pltpu.SemaphoreType.DMA((chips, subs)),
            pltpu.SemaphoreType.DMA((chips, subs)),
            pltpu.SemaphoreType.DMA((chips, subs)),
            pltpu.SemaphoreType.DMA((2,)),
            pltpu.SemaphoreType.DMA((2,)),
        ],
        compiler_params=pltpu.CompilerParams(
            vmem_limit_bytes=VMEM_LIMIT, collective_id=0, has_side_effects=True
        ),
        cost_estimate=pl.CostEstimate(
            flops=8 * freq_count * local * sources * lanes,
            bytes_accessed=2 * rows * samples + 4 * freq_count * local * sources,
            transcendentals=0,
        ),
    )(traces2, table, tiled)


def finish_kernel(freq_count, shots, points, near_ref, lines, basis_ref, traces_ref, out_ref, split_basis):
    step = pl.program_id(0)
    lanes = 2 * shots
    terms = 2 * freq_count

    @pl.when(step == 0)
    def _():
        basis = basis_ref[...]
        high = basis.astype(jnp.bfloat16)
        split_basis[0:terms, :] = high
        split_basis[terms : 2 * terms, :] = high
        split_basis[2 * terms :, :] = (basis - high.astype(jnp.float32)).astype(jnp.bfloat16)

    start = step * points
    low = lax.broadcasted_iota(jnp.int32, (freq_count, lanes), 1) < shots

    def mixed(point):
        own = pl.multiple_of((point + HALO) * freq_count, freq_count)
        other = pl.multiple_of((point + HALO + near_ref[point]) * freq_count, freq_count)
        return lines[pl.ds(own, freq_count), :] + 0.5 * lines[pl.ds(other, freq_count), :]

    group = 8
    for part in range(points // group):
        reals, imags = [], []
        for two in range(group // 2):
            first = mixed(start + part * group + 2 * two)
            second = mixed(start + part * group + 2 * two + 1)
            reals.append(jnp.where(low, first, swap_halves(second, shots)))
            imags.append(jnp.where(low, swap_halves(first, shots), second))
        terms_by_row = jnp.concatenate(
            [jnp.concatenate(reals, axis=1), jnp.concatenate(imags, axis=1)], axis=0
        )
        high = terms_by_row.astype(jnp.bfloat16)
        rest = (terms_by_row - high.astype(jnp.float32)).astype(jnp.bfloat16)
        left = jnp.concatenate([high, rest, high], axis=0)
        adapted = lax.dot_general(
            left, split_basis[...], TN_DIMS, preferred_element_type=jnp.float32
        )
        rows = slice(part * group * shots, (part + 1) * group * shots)
        out_ref[rows, :] = (traces_ref[rows, :].astype(jnp.float32) - adapted).astype(out_ref.dtype)


def finish(near, lines, basis, traces2, freq_count, shots, local, points):
    rows, samples = traces2.shape
    block = points * shots
    return pl.pallas_call(
        functools.partial(finish_kernel, freq_count, shots, points),
        out_shape=jax.ShapeDtypeStruct((rows, samples), jnp.bfloat16),
        grid=(local // points,),
        in_specs=[
            pl.BlockSpec(memory_space=pltpu.SMEM),
            pl.BlockSpec(lines.shape, lambda i: (0, 0)),
            pl.BlockSpec((2 * freq_count, samples), lambda i: (0, 0)),
            pl.BlockSpec((block, samples), lambda i: (i, 0)),
        ],
        out_specs=pl.BlockSpec((block, samples), lambda i: (i, 0)),
        scratch_shapes=[pltpu.VMEM((6 * freq_count, samples), jnp.bfloat16)],
        compiler_params=pltpu.CompilerParams(
            vmem_limit_bytes=VMEM_LIMIT, dimension_semantics=("arbitrary",)
        ),
        cost_estimate=pl.CostEstimate(
            flops=12 * freq_count * rows * samples, bytes_accessed=4 * rows * samples, transcendentals=0
        ),
    )(near, lines, basis, traces2)


def on_device(traces, operator, freq_bins, win_lengths, coefficients, neighbour):
    local, shots, samples = traces.shape
    freq_count = freq_bins.shape[0]
    size = lax.axis_size("surf")
    points = 32
    angles = angle_grid(freq_bins, samples)
    table = jnp.concatenate([jnp.cos(angles.T), -jnp.sin(angles.T)], axis=0)
    norm = (2.0 * freq_count * samples) ** (-0.5)
    basis = matching(norm * table, coefficients, win_lengths)
    traces2 = traces.reshape(local * shots, samples)
    bf16_table = table.astype(jnp.bfloat16)
    subs, step_points = 4, 16
    if size % 4 == 0 and local % (2 * BF16_LANES) == 0 and size % (local // step_points) == 0:
        lines = predict(
            traces2, bf16_table, operator, freq_count, shots, local, size, step_points, subs
        )
        out = finish(neighbour, lines, basis, traces2, freq_count, shots, local, points)
        return out.reshape(local, shots, samples)

    up = [(i, i + 1) for i in range(size - 1)]
    down = [(j, i) for i, j in up]
    before = lax.ppermute(operator[local - HALO :], "surf", up)
    after = lax.ppermute(operator[:HALO], "surf", down)
    edge = jnp.concatenate([before, after], axis=0).transpose(1, 2, 0, 3)
    edge = jnp.pad(edge, ((0, 0), (0, 0), (0, 8 - 2 * HALO), (0, 0)))
    edge = edge.reshape(freq_count, 16, operator.shape[3])

    chunks = 1
    gathered = []
    for chunk in range(chunks):
        spectra = forward(traces2, bf16_table, freq_count, shots, points, chunk, chunks)
        gathered.append(lax.all_gather(spectra, "surf"))
    by_freq = operator.transpose(1, 2, 0, 3)
    partial = []
    for chunk in range(chunks - 1):
        partial.append(partial_product(by_freq, edge, gathered[chunk], shots, chunk, chunks))
    out = adapt(
        neighbour, by_freq, edge, gathered[-1], partial, basis, traces2,
        shots, points, chunks - 1, chunks,
    )
    return out.reshape(local, shots, samples)


def solution(mesh):
    return jax.shard_map(
        on_device,
        mesh=mesh,
        in_specs=(P("surf", "group", None), P("surf", None, None, None), P(), P(), P(), P("surf")),
        out_specs=P("surf", "group", None),
        check_vma=False,
    )
```

```python
import functools
import math

import jax
import jax.numpy as jnp
from jax import lax
from jax.experimental import pallas as pl
from jax.experimental.pallas import tpu as pltpu
from jax.sharding import PartitionSpec as P

TAPS = 31
HALO = 2
VMEM_LIMIT = 60 * 1024 * 1024
PREDICT_VMEM = 27 * 1024 * 1024
FINISH_VMEM = 24 * 1024 * 1024
NT_DIMS = (((1,), (1,)), ((), ()))
TN_DIMS = (((0,), (0,)), ((), ()))


def angle_grid(freq_bins, samples):
    sample_index = jnp.arange(samples, dtype=jnp.int32)
    phases = sample_index[:, None] * freq_bins[None, :] % samples
    return 2.0 * math.pi / samples * phases.astype(jnp.float32)


def matching(multiple_estimate, coefficients, win_lengths):
    samples = multiple_estimate.shape[1]
    half_taps = (TAPS - 1) // 2
    order = jnp.arange(win_lengths.shape[0], dtype=jnp.int32)
    window_ends = jnp.sum(jnp.where(order[:, None] <= order[None, :], win_lengths[:, None], 0), axis=0)
    sample_index = jnp.arange(samples, dtype=jnp.int32)
    window = jnp.sum((window_ends[None, :] <= sample_index[:, None]).astype(jnp.int32), axis=1)
    membership = (
        window[None, :] == jnp.arange(coefficients.shape[0], dtype=jnp.int32)[:, None]
    ).astype(jnp.float32)
    per_sample = jnp.dot(coefficients.T, membership, precision=lax.Precision.HIGHEST)
    padded = jnp.pad(multiple_estimate, ((0, 0), (half_taps, half_taps)))
    summed = jnp.zeros_like(multiple_estimate)
    for lag_index in range(TAPS):
        summed = summed + per_sample[lag_index][None] * padded[:, lag_index : lag_index + samples]
    return summed


def swap_halves(x, half):
    return pltpu.roll(x, half, axis=1)


def forward_kernel(freq_count, shots, traces_ref, table_ref, out_ref, lines):
    points = out_ref.shape[1]
    lanes = 2 * shots
    spectra = lax.dot_general(
        table_ref[...], traces_ref[...], NT_DIMS, preferred_element_type=jnp.float32
    )
    low = lax.broadcasted_iota(jnp.int32, (freq_count, lanes), 1) < shots
    for pair in range(points // 2):
        cols = slice(pair * lanes, (pair + 1) * lanes)
        real, imag = spectra[:freq_count, cols], spectra[freq_count:, cols]
        first = jnp.where(low, real, swap_halves(imag, shots))
        second = jnp.where(low, swap_halves(real, shots), imag)
        at = 2 * pair * freq_count
        lines[at : at + freq_count, :] = first
        lines[at + freq_count : at + 2 * freq_count, :] = second
    for f in range(freq_count):
        out_ref[f] = lines[pl.ds(f, points, stride=freq_count), :].astype(out_ref.dtype)


def forward(traces2, table, freq_count, shots, points, chunk, chunks):
    rows, samples = traces2.shape
    rows = rows // chunks
    local = rows // shots
    first = chunk * (local // points)
    return pl.pallas_call(
        functools.partial(forward_kernel, freq_count, shots),
        out_shape=jax.ShapeDtypeStruct((freq_count, local, 2 * shots), jnp.bfloat16),
        grid=(local // points,),
        in_specs=[
            pl.BlockSpec((points * shots, samples), lambda i: (first + i, 0)),
            pl.BlockSpec((2 * freq_count, samples), lambda i: (0, 0)),
        ],
        out_specs=pl.BlockSpec((freq_count, points, 2 * shots), lambda i: (0, i, 0)),
        scratch_shapes=[pltpu.VMEM((points * freq_count, 2 * shots), jnp.float32)],
        compiler_params=pltpu.CompilerParams(
            vmem_limit_bytes=VMEM_LIMIT, dimension_semantics=("arbitrary",)
        ),
        cost_estimate=pl.CostEstimate(
            flops=4 * freq_count * rows * samples,
            bytes_accessed=2 * rows * samples,
            transcendentals=0,
        ),
    )(traces2, table)


def combined(real_rows, imag_rows, shots):
    low = lax.broadcasted_iota(jnp.int32, real_rows.shape, 1) < shots
    return real_rows + jnp.where(low, -1.0, 1.0) * swap_halves(imag_rows, shots)


def products(operator_refs, edge_refs, spectra_ref, shots):
    spectra = spectra_ref[:, 0].reshape(-1, 2 * shots)
    planes = [
        jnp.concatenate([ref[0, part] for ref in operator_refs], axis=1) for part in range(2)
    ]
    planes.append(jnp.concatenate([ref[0] for ref in edge_refs], axis=1))
    real, imag, edge = [
        jnp.dot(plane, spectra, preferred_element_type=jnp.float32) for plane in planes
    ]
    return combined(real, imag, shots), combined(edge[0:8], edge[8:16], shots)


def partial_kernel(shots, pieces, *refs):
    operator_refs, edge_refs = refs[:pieces], refs[pieces : 2 * pieces]
    spectra_ref, out_ref = refs[2 * pieces :]
    local = operator_refs[0].shape[2]
    main, edge = products(operator_refs, edge_refs, spectra_ref, shots)
    out_ref[0, 8 : 8 + local, :] = main
    out_ref[0, 0:8, :] = edge


def source_specs(local, sources, parts, chunk, chunks, f_of):
    pieces = parts if chunks > 1 else 1
    width = sources // (pieces * chunks)

    def column(piece):
        return piece * chunks + chunk

    operator_specs = [
        pl.BlockSpec((1, 2, local, width), lambda i, c=column(p): (f_of(i), 0, 0, c))
        for p in range(pieces)
    ]
    edge_specs = [
        pl.BlockSpec((1, 16, width), lambda i, c=column(p): (f_of(i), 0, c))
        for p in range(pieces)
    ]
    return pieces, operator_specs, edge_specs


def partial_product(operator, edge, spectra, shots, chunk, chunks):
    freq_count, _, local, sources = operator.shape
    parts, _, mine, lanes = spectra.shape
    pieces, operator_specs, edge_specs = source_specs(
        local, sources, parts, chunk, chunks, lambda i: i
    )
    return pl.pallas_call(
        functools.partial(partial_kernel, shots, pieces),
        out_shape=jax.ShapeDtypeStruct((freq_count, local + 8, lanes), jnp.float32),
        grid=(freq_count,),
        in_specs=operator_specs
        + edge_specs
        + [pl.BlockSpec((parts, 1, mine, lanes), lambda i: (0, i, 0, 0))],
        out_specs=pl.BlockSpec((1, local + 8, lanes), lambda i: (i, 0, 0)),
        compiler_params=pltpu.CompilerParams(
            vmem_limit_bytes=VMEM_LIMIT, dimension_semantics=("arbitrary",)
        ),
        cost_estimate=pl.CostEstimate(
            flops=4 * freq_count * local * (sources // chunks) * lanes,
            bytes_accessed=4 * freq_count * local * (sources // chunks),
            transcendentals=0,
        ),
    )(*([operator] * pieces), *([edge] * pieces), spectra)


def adapt_kernel(freq_count, shots, points, pieces, partials, *refs):
    near_ref, operator_refs, edge_refs = refs[0], refs[1 : 1 + pieces], refs[1 + pieces : 1 + 2 * pieces]
    spectra_ref = refs[1 + 2 * pieces]
    partial_refs = refs[2 + 2 * pieces : 2 + 2 * pieces + partials]
    basis_ref, traces_ref, out_ref, predicted, lines, split_basis = refs[2 + 2 * pieces + partials :]
    step = pl.program_id(0)
    local = operator_refs[0].shape[2]
    lanes = 2 * shots
    terms = 2 * freq_count

    @pl.when(step == 0)
    def _():
        basis = basis_ref[...]
        high = basis.astype(jnp.bfloat16)
        split_basis[0:terms, :] = high
        split_basis[terms : 2 * terms, :] = high
        split_basis[2 * terms :, :] = (basis - high.astype(jnp.float32)).astype(jnp.bfloat16)

    @pl.when(step < freq_count)
    def _():
        main, edge = products(operator_refs, edge_refs, spectra_ref, shots)
        for ref in partial_refs:
            main = main + ref[0, 8 : 8 + local, :]
            edge = edge + ref[0, 0:8, :]
        predicted[step, 8 : 8 + local, :] = main
        predicted[step, 0:8, :] = edge

    @pl.when(step == freq_count - 1)
    def _():
        for f in range(freq_count):
            mine = predicted[f, 8 : 8 + local, :]
            lines[pl.ds(HALO * freq_count + f, local, stride=freq_count), :] = mine
            for h in range(HALO):
                before = h * freq_count + f
                lines[before : before + 1, :] = predicted[f, h : h + 1, :]
                after = (HALO + local + h) * freq_count + f
                lines[after : after + 1, :] = predicted[f, HALO + h : HALO + h + 1, :]

    @pl.when(step >= freq_count)
    def _():
        start = (step - freq_count) * points
        low = lax.broadcasted_iota(jnp.int32, (freq_count, lanes), 1) < shots

        def mixed(point):
            own = pl.multiple_of((point + HALO) * freq_count, freq_count)
            other = pl.multiple_of((point + HALO + near_ref[point]) * freq_count, freq_count)
            return lines[pl.ds(own, freq_count), :] + 0.5 * lines[pl.ds(other, freq_count), :]

        group = 8
        for part in range(points // group):
            reals, imags = [], []
            for pair in range(group // 2):
                first = mixed(start + part * group + 2 * pair)
                second = mixed(start + part * group + 2 * pair + 1)
                reals.append(jnp.where(low, first, swap_halves(second, shots)))
                imags.append(jnp.where(low, swap_halves(first, shots), second))
            terms_by_row = jnp.concatenate(
                [jnp.concatenate(reals, axis=1), jnp.concatenate(imags, axis=1)], axis=0
            )
            high = terms_by_row.astype(jnp.bfloat16)
            rest = (terms_by_row - high.astype(jnp.float32)).astype(jnp.bfloat16)
            left = jnp.concatenate([high, rest, high], axis=0)
            adapted = lax.dot_general(
                left, split_basis[...], TN_DIMS, preferred_element_type=jnp.float32
            )
            rows = slice(part * group * shots, (part + 1) * group * shots)
            out_ref[rows, :] = (traces_ref[rows, :].astype(jnp.float32) - adapted).astype(
                out_ref.dtype
            )


def adapt(near, operator, edge, spectra, partial, basis, traces2, shots, points, chunk, chunks):
    freq_count, _, local, sources = operator.shape
    rows, samples = traces2.shape
    parts, _, mine, lanes = spectra.shape
    block = points * shots

    def f_of(i):
        return jnp.minimum(i, freq_count - 1)

    def row_of(i):
        return jnp.maximum(i - freq_count, 0)

    pieces, operator_specs, edge_specs = source_specs(local, sources, parts, chunk, chunks, f_of)
    partial_specs = [
        pl.BlockSpec((1, local + 8, lanes), lambda i: (f_of(i), 0, 0)) for _ in partial
    ]
    return pl.pallas_call(
        functools.partial(adapt_kernel, freq_count, shots, points, pieces, len(partial)),
        out_shape=jax.ShapeDtypeStruct((rows, samples), jnp.bfloat16),
        grid=(freq_count + local // points,),
        in_specs=[pl.BlockSpec(memory_space=pltpu.SMEM)]
        + operator_specs
        + edge_specs
        + [pl.BlockSpec((parts, 1, mine, lanes), lambda i: (0, f_of(i), 0, 0))]
        + partial_specs
        + [
            pl.BlockSpec((2 * freq_count, samples), lambda i: (0, 0)),
            pl.BlockSpec((block, samples), lambda i: (row_of(i), 0)),
        ],
        out_specs=pl.BlockSpec((block, samples), lambda i: (row_of(i), 0)),
        scratch_shapes=[
            pltpu.VMEM((freq_count, local + 8, lanes), jnp.float32),
            pltpu.VMEM(((local + 2 * HALO) * freq_count, lanes), jnp.float32),
            pltpu.VMEM((6 * freq_count, samples), jnp.bfloat16),
        ],
        compiler_params=pltpu.CompilerParams(
            vmem_limit_bytes=VMEM_LIMIT, dimension_semantics=("arbitrary",)
        ),
    )(near, *([operator] * pieces), *([edge] * pieces), spectra, *partial, basis, traces2)


MESH = pl.DeviceIdType.MESH
BF16_LANES = 128


def place(size):
    me = lax.axis_index("surf")
    chips = size // 2
    chip, core = me // 2, me % 2
    position = jnp.where(chip % 2 == 0, chip // 2, chips - 1 - chip // 2)
    return me, core, position, 1 - 2 * core


def device_at(position, core, chips):
    position = (position + chips) % chips
    chip = jnp.where(position < chips // 2, 2 * position, 2 * (chips - 1 - position) + 1)
    return 2 * chip + core


def predict_kernel(
    size, freq_count, shots, local, points, subs, *refs
):
    traces, table, operator, held, lines = refs[:5]
    held_sem, planes, planes_sem, spectra, total, rows = refs[5:11]
    edge_out, edge_in = refs[11:13]
    ring_send, ring_recv, pair_send, pair_recv, edge_send, edge_recv = refs[13:]
    chips = size // 2
    lanes = 2 * shots
    me, core, position, toward = place(size)
    pair = me + 1 - 2 * core
    after = device_at(position + toward, core, chips)
    before = device_at(position - toward, core, chips)
    beside = (me + 2 * core - 1 + size) % size
    tiles = local // BF16_LANES
    chunks = local // points
    sub_points = local // subs
    per_sub = chunks // subs
    slots = planes.shape[0]
    early = min(slots, chunks)
    block_rows = points * shots

    def origin(step, which):
        sign = toward * (1 - 2 * which)
        return device_at(position - step * sign, core + which - 2 * core * which, chips)

    def held_rows(chunk):
        return pl.ds(pl.multiple_of(chunk * block_rows, block_rows), block_rows)

    def held_copy(chunk):
        at = held_rows(chunk)
        return pltpu.make_async_copy(traces.at[at], held.at[at], held_sem.at[chunk])

    def fetch_planes(order):
        dev, slot = origin(order // 2, order % 2), order % slots

        def one(f, carry):
            for tile in range(tiles):
                pltpu.make_async_copy(
                    operator.at[:, f, dev * tiles + tile], planes.at[slot, f, tile], planes_sem.at[slot]
                ).start()
            return carry

        lax.fori_loop(0, freq_count, one, 0)

    def part(dev, sub):
        return spectra.at[dev, :, pl.ds(pl.multiple_of(sub * sub_points, sub_points), sub_points), :]

    def ring_copy(step, sub):
        ref = part(origin(step, 0), sub)
        return pltpu.make_async_remote_copy(
            ref, ref, ring_send.at[step, sub], ring_recv.at[step + 1, sub],
            device_id={"surf": after}, device_id_type=MESH,
        )

    def pair_copy(step, sub):
        ref = part(origin(step, 0), sub)
        return pltpu.make_async_remote_copy(
            ref, ref, pair_send.at[step, sub], pair_recv.at[step, sub],
            device_id={"surf": pair}, device_id_type=MESH,
        )

    def arrive(step, sub):
        ref = part(origin(step, 0), sub)
        pltpu.make_async_remote_copy(
            ref, ref, ring_send.at[step - 1, sub], ring_recv.at[step, sub],
            device_id={"surf": after}, device_id_type=MESH,
        ).wait_recv()

    def arrive_pair(step, sub):
        ref = part(origin(step, 1), sub)
        pltpu.make_async_remote_copy(
            ref, ref, pair_send.at[step, sub], pair_recv.at[step, sub],
            device_id={"surf": pair}, device_id_type=MESH,
        ).wait_recv()

    def product(order):
        dev = origin(order // 2, order % 2)
        slot = order % slots
        block = planes.at[slot]
        pltpu.make_async_copy(block, block, planes_sem.at[slot]).wait()
        flat = planes.reshape(slots, freq_count, tiles, 2 * local, BF16_LANES)
        for f in range(freq_count):
            left = jnp.concatenate([flat[slot, f, tile] for tile in range(tiles)], axis=1)
            total[f] += jnp.dot(left, spectra[dev, f], preferred_element_type=jnp.float32)

        @pl.when(order + early < size)
        def _():
            fetch_planes(order + early)

    def begin(chunk, carry):
        held_copy(chunk).start()
        return carry

    lax.fori_loop(0, chunks, begin, 0)

    barrier = pltpu.get_barrier_semaphore()
    for other in (after, before, pair, beside):
        pl.semaphore_signal(barrier, inc=1, device_id={"surf": other}, device_id_type=MESH)
    total[...] = jnp.zeros_like(total)
    pl.semaphore_wait(barrier, 4)

    low = lax.broadcasted_iota(jnp.int32, (freq_count, lanes), 1) < shots

    def forward(chunk, carry):
        @pl.when(chunk >= chunks - early)
        def _():
            fetch_planes(chunk - (chunks - early))

        held_copy(chunk).wait()
        found = lax.dot_general(
            table[...], held[held_rows(chunk), :], NT_DIMS, preferred_element_type=jnp.float32
        )
        for two in range(points // 2):
            cols = slice(two * lanes, (two + 1) * lanes)
            real, imag = found[:freq_count, cols], found[freq_count:, cols]
            first = jnp.where(low, real, swap_halves(imag, shots))
            second = jnp.where(low, swap_halves(real, shots), imag)
            at = 2 * two * freq_count
            rows[at : at + freq_count, :] = first
            rows[at + freq_count : at + 2 * freq_count, :] = second
        start = pl.multiple_of(chunk * points, points)
        for f in range(freq_count):
            spectra[me, f, pl.ds(start, points), :] = rows[
                pl.ds(f, points, stride=freq_count), :
            ].astype(spectra.dtype)
        return carry

    for sub in range(subs):
        lax.fori_loop(sub * per_sub, (sub + 1) * per_sub, forward, 0)
        for older in range(sub, -1, -1):
            step = sub - older
            if step <= chips - 1:
                if step > 0:
                    arrive(step, older)
                if step < chips - 1:
                    ring_copy(step, older).start()
                pair_copy(step, older).start()

    def both(step):
        product(2 * step)
        for sub in range(subs):
            arrive_pair(step, sub)
        product(2 * step + 1)

    def onward(front, carry):
        both(front - subs)
        for sub in range(subs - 1, -1, -1):
            step = front - sub

            @pl.when(step <= chips - 1)
            def _():
                arrive(step, sub)

                @pl.when(step < chips - 1)
                def _():
                    ring_copy(step, sub).start()

                pair_copy(step, sub).start()

        return carry

    lax.fori_loop(subs, chips + subs - 1, onward, 0)
    both(chips - 1)

    low_all = lax.broadcasted_iota(jnp.int32, (local, lanes), 1) < shots
    sign = jnp.where(low_all, -1.0, 1.0)
    for f in range(freq_count):
        real = total[f, pl.ds(0, local, stride=2), :]
        imag = total[f, pl.ds(1, local, stride=2), :]
        lines[pl.ds(HALO * freq_count + f, local, stride=freq_count), :] = (
            real + sign * swap_halves(imag, shots)
        )
    width = HALO * freq_count
    edge_out[0] = lines[width : 2 * width, :]
    edge_out[1] = lines[local * freq_count : local * freq_count + width, :]

    def edge_copy(which, to):
        return pltpu.make_async_remote_copy(
            edge_out.at[which], edge_in.at[1 - which], edge_send.at[which], edge_recv.at[1 - which],
            device_id={"surf": to}, device_id_type=MESH,
        )

    previous, following = (me + size - 1) % size, (me + 1) % size
    edges = [edge_copy(0, previous), edge_copy(1, following)]
    for copy in edges:
        copy.start()
    for copy in edges:
        copy.wait()
    lines[0:width, :] = jnp.where(me > 0, edge_in[0], 0.0)
    lines[width + local * freq_count :, :] = jnp.where(me < size - 1, edge_in[1], 0.0)

    def drain(step, carry):
        for sub in range(subs):
            @pl.when(step < chips - 1)
            def _():
                ring_copy(step, sub).wait_send()

            pair_copy(step, sub).wait_send()
        return carry

    lax.fori_loop(0, chips, drain, 0)


def predict(traces2, table, operator, freq_count, shots, local, size, points, subs):
    rows, samples = traces2.shape
    sources = operator.shape[3]
    lanes = 2 * shots
    tiles = sources // BF16_LANES
    tiled = operator.reshape(local, freq_count, 2, tiles, BF16_LANES).transpose(0, 1, 3, 2, 4)
    chips = size // 2
    slots = 6
    width = HALO * freq_count
    return pl.pallas_call(
        functools.partial(predict_kernel, size, freq_count, shots, local, points, subs),
        out_shape=[
            pltpu.VMEM((rows, samples), jnp.bfloat16),
            jax.ShapeDtypeStruct(((local + 2 * HALO) * freq_count, lanes), jnp.float32),
        ],
        in_specs=[
            pl.BlockSpec(memory_space=pl.ANY),
            pl.BlockSpec(memory_space=pltpu.VMEM),
            pl.BlockSpec(memory_space=pl.ANY),
        ],
        out_specs=[pl.BlockSpec(memory_space=pltpu.VMEM)] * 2,
        scratch_shapes=[
            pltpu.SemaphoreType.DMA((local // points,)),
            pltpu.VMEM((slots, freq_count, local // BF16_LANES, local, 2, BF16_LANES), jnp.bfloat16),
            pltpu.SemaphoreType.DMA((slots,)),
            pltpu.VMEM((size, freq_count, local, lanes), jnp.bfloat16),
            pltpu.VMEM((freq_count, 2 * local, lanes), jnp.float32),
            pltpu.VMEM((points * freq_count, lanes), jnp.float32),
            pltpu.VMEM((2, width, lanes), jnp.float32),
            pltpu.VMEM((2, width, lanes), jnp.float32),
            pltpu.SemaphoreType.DMA((chips, subs)),
            pltpu.SemaphoreType.DMA((chips, subs)),
            pltpu.SemaphoreType.DMA((chips, subs)),
            pltpu.SemaphoreType.DMA((chips, subs)),
            pltpu.SemaphoreType.DMA((2,)),
            pltpu.SemaphoreType.DMA((2,)),
        ],
        compiler_params=pltpu.CompilerParams(
            vmem_limit_bytes=PREDICT_VMEM, collective_id=0, has_side_effects=True
        ),
        cost_estimate=pl.CostEstimate(
            flops=8 * freq_count * local * sources * lanes,
            bytes_accessed=2 * rows * samples + 4 * freq_count * local * sources,
            transcendentals=0,
        ),
    )(traces2, table, tiled)


def finish_kernel(freq_count, shots, points, near_ref, lines, basis_ref, traces_ref, out_ref, split_basis):
    step = pl.program_id(0)
    lanes = 2 * shots
    terms = 2 * freq_count

    @pl.when(step == 0)
    def _():
        basis = basis_ref[...]
        high = basis.astype(jnp.bfloat16)
        split_basis[0:terms, :] = high
        split_basis[terms : 2 * terms, :] = high
        split_basis[2 * terms :, :] = (basis - high.astype(jnp.float32)).astype(jnp.bfloat16)

    start = step * points
    low = lax.broadcasted_iota(jnp.int32, (freq_count, lanes), 1) < shots

    def mixed(point):
        own = pl.multiple_of((point + HALO) * freq_count, freq_count)
        other = pl.multiple_of((point + HALO + near_ref[point]) * freq_count, freq_count)
        return lines[pl.ds(own, freq_count), :] + 0.5 * lines[pl.ds(other, freq_count), :]

    group = 8
    for part in range(points // group):
        reals, imags = [], []
        for two in range(group // 2):
            first = mixed(start + part * group + 2 * two)
            second = mixed(start + part * group + 2 * two + 1)
            reals.append(jnp.where(low, first, swap_halves(second, shots)))
            imags.append(jnp.where(low, swap_halves(first, shots), second))
        terms_by_row = jnp.concatenate(
            [jnp.concatenate(reals, axis=1), jnp.concatenate(imags, axis=1)], axis=0
        )
        high = terms_by_row.astype(jnp.bfloat16)
        rest = (terms_by_row - high.astype(jnp.float32)).astype(jnp.bfloat16)
        left = jnp.concatenate([high, rest, high], axis=0)
        adapted = lax.dot_general(
            left, split_basis[...], TN_DIMS, preferred_element_type=jnp.float32
        )
        rows = slice(part * group * shots, (part + 1) * group * shots)
        held = pl.ds(pl.multiple_of((start + part * group) * shots, group * shots), group * shots)
        out_ref[rows, :] = (traces_ref[held, :].astype(jnp.float32) - adapted).astype(out_ref.dtype)


def finish(near, lines, basis, traces2, freq_count, shots, local, points):
    rows, samples = traces2.shape
    block = points * shots
    return pl.pallas_call(
        functools.partial(finish_kernel, freq_count, shots, points),
        out_shape=jax.ShapeDtypeStruct((rows, samples), jnp.bfloat16),
        grid=(local // points,),
        in_specs=[
            pl.BlockSpec(memory_space=pltpu.SMEM),
            pl.BlockSpec(memory_space=pltpu.VMEM),
            pl.BlockSpec((2 * freq_count, samples), lambda i: (0, 0)),
            pl.BlockSpec(memory_space=pltpu.VMEM),
        ],
        out_specs=pl.BlockSpec((block, samples), lambda i: (i, 0)),
        scratch_shapes=[pltpu.VMEM((6 * freq_count, samples), jnp.bfloat16)],
        compiler_params=pltpu.CompilerParams(
            vmem_limit_bytes=FINISH_VMEM, dimension_semantics=("arbitrary",)
        ),
        cost_estimate=pl.CostEstimate(
            flops=12 * freq_count * rows * samples, bytes_accessed=4 * rows * samples, transcendentals=0
        ),
    )(near, lines, basis, traces2)


def on_device(traces, operator, freq_bins, win_lengths, coefficients, neighbour):
    local, shots, samples = traces.shape
    freq_count = freq_bins.shape[0]
    size = lax.axis_size("surf")
    points = 32
    angles = angle_grid(freq_bins, samples)
    table = jnp.concatenate([jnp.cos(angles.T), -jnp.sin(angles.T)], axis=0)
    norm = (2.0 * freq_count * samples) ** (-0.5)
    basis = matching(norm * table, coefficients, win_lengths)
    traces2 = traces.reshape(local * shots, samples)
    bf16_table = table.astype(jnp.bfloat16)
    subs, step_points = 4, 16
    if size % 4 == 0 and local % (2 * BF16_LANES) == 0:
        held, lines = predict(
            traces2, bf16_table, operator, freq_count, shots, local, size, step_points, subs
        )
        held = pltpu.with_memory_space_constraint(held, pltpu.VMEM)
        out = finish(neighbour, lines, basis, held, freq_count, shots, local, points)
        return out.reshape(local, shots, samples)

    up = [(i, i + 1) for i in range(size - 1)]
    down = [(j, i) for i, j in up]
    before = lax.ppermute(operator[local - HALO :], "surf", up)
    after = lax.ppermute(operator[:HALO], "surf", down)
    edge = jnp.concatenate([before, after], axis=0).transpose(1, 2, 0, 3)
    edge = jnp.pad(edge, ((0, 0), (0, 0), (0, 8 - 2 * HALO), (0, 0)))
    edge = edge.reshape(freq_count, 16, operator.shape[3])

    chunks = 1
    gathered = []
    for chunk in range(chunks):
        spectra = forward(traces2, bf16_table, freq_count, shots, points, chunk, chunks)
        gathered.append(lax.all_gather(spectra, "surf"))
    by_freq = operator.transpose(1, 2, 0, 3)
    partial = []
    for chunk in range(chunks - 1):
        partial.append(partial_product(by_freq, edge, gathered[chunk], shots, chunk, chunks))
    out = adapt(
        neighbour, by_freq, edge, gathered[-1], partial, basis, traces2,
        shots, points, chunks - 1, chunks,
    )
    return out.reshape(local, shots, samples)


def solution(mesh):
    return jax.shard_map(
        on_device,
        mesh=mesh,
        in_specs=(P("surf", "group", None), P("surf", None, None, None), P(), P(), P(), P("surf")),
        out_specs=P("surf", "group", None),
        check_vma=False,
    )
```

```python
import functools
import math

import jax
import jax.numpy as jnp
from jax import lax
from jax.experimental import pallas as pl
from jax.experimental.pallas import tpu as pltpu
from jax.sharding import PartitionSpec as P

TAPS = 31
HALO = 2
VMEM_LIMIT = 60 * 1024 * 1024
PREDICT_VMEM = 27 * 1024 * 1024
FINISH_VMEM = 24 * 1024 * 1024
NT_DIMS = (((1,), (1,)), ((), ()))
TN_DIMS = (((0,), (0,)), ((), ()))


def angle_grid(freq_bins, samples):
    sample_index = jnp.arange(samples, dtype=jnp.int32)
    phases = sample_index[:, None] * freq_bins[None, :] % samples
    return 2.0 * math.pi / samples * phases.astype(jnp.float32)


def matching(multiple_estimate, coefficients, win_lengths):
    samples = multiple_estimate.shape[1]
    half_taps = (TAPS - 1) // 2
    order = jnp.arange(win_lengths.shape[0], dtype=jnp.int32)
    window_ends = jnp.sum(jnp.where(order[:, None] <= order[None, :], win_lengths[:, None], 0), axis=0)
    sample_index = jnp.arange(samples, dtype=jnp.int32)
    window = jnp.sum((window_ends[None, :] <= sample_index[:, None]).astype(jnp.int32), axis=1)
    membership = (
        window[None, :] == jnp.arange(coefficients.shape[0], dtype=jnp.int32)[:, None]
    ).astype(jnp.float32)
    per_sample = jnp.dot(coefficients.T, membership, precision=lax.Precision.HIGHEST)
    padded = jnp.pad(multiple_estimate, ((0, 0), (half_taps, half_taps)))
    summed = jnp.zeros_like(multiple_estimate)
    for lag_index in range(TAPS):
        summed = summed + per_sample[lag_index][None] * padded[:, lag_index : lag_index + samples]
    return summed


def swap_halves(x, half):
    return pltpu.roll(x, half, axis=1)


def forward_kernel(freq_count, shots, traces_ref, table_ref, out_ref, lines):
    points = out_ref.shape[1]
    lanes = 2 * shots
    spectra = lax.dot_general(
        table_ref[...], traces_ref[...], NT_DIMS, preferred_element_type=jnp.float32
    )
    low = lax.broadcasted_iota(jnp.int32, (freq_count, lanes), 1) < shots
    for pair in range(points // 2):
        cols = slice(pair * lanes, (pair + 1) * lanes)
        real, imag = spectra[:freq_count, cols], spectra[freq_count:, cols]
        first = jnp.where(low, real, swap_halves(imag, shots))
        second = jnp.where(low, swap_halves(real, shots), imag)
        at = 2 * pair * freq_count
        lines[at : at + freq_count, :] = first
        lines[at + freq_count : at + 2 * freq_count, :] = second
    for f in range(freq_count):
        out_ref[f] = lines[pl.ds(f, points, stride=freq_count), :].astype(out_ref.dtype)


def forward(traces2, table, freq_count, shots, points, chunk, chunks):
    rows, samples = traces2.shape
    rows = rows // chunks
    local = rows // shots
    first = chunk * (local // points)
    return pl.pallas_call(
        functools.partial(forward_kernel, freq_count, shots),
        out_shape=jax.ShapeDtypeStruct((freq_count, local, 2 * shots), jnp.bfloat16),
        grid=(local // points,),
        in_specs=[
            pl.BlockSpec((points * shots, samples), lambda i: (first + i, 0)),
            pl.BlockSpec((2 * freq_count, samples), lambda i: (0, 0)),
        ],
        out_specs=pl.BlockSpec((freq_count, points, 2 * shots), lambda i: (0, i, 0)),
        scratch_shapes=[pltpu.VMEM((points * freq_count, 2 * shots), jnp.float32)],
        compiler_params=pltpu.CompilerParams(
            vmem_limit_bytes=VMEM_LIMIT, dimension_semantics=("arbitrary",)
        ),
        cost_estimate=pl.CostEstimate(
            flops=4 * freq_count * rows * samples,
            bytes_accessed=2 * rows * samples,
            transcendentals=0,
        ),
    )(traces2, table)


def combined(real_rows, imag_rows, shots):
    low = lax.broadcasted_iota(jnp.int32, real_rows.shape, 1) < shots
    return real_rows + jnp.where(low, -1.0, 1.0) * swap_halves(imag_rows, shots)


def products(operator_refs, edge_refs, spectra_ref, shots):
    spectra = spectra_ref[:, 0].reshape(-1, 2 * shots)
    planes = [
        jnp.concatenate([ref[0, part] for ref in operator_refs], axis=1) for part in range(2)
    ]
    planes.append(jnp.concatenate([ref[0] for ref in edge_refs], axis=1))
    real, imag, edge = [
        jnp.dot(plane, spectra, preferred_element_type=jnp.float32) for plane in planes
    ]
    return combined(real, imag, shots), combined(edge[0:8], edge[8:16], shots)


def partial_kernel(shots, pieces, *refs):
    operator_refs, edge_refs = refs[:pieces], refs[pieces : 2 * pieces]
    spectra_ref, out_ref = refs[2 * pieces :]
    local = operator_refs[0].shape[2]
    main, edge = products(operator_refs, edge_refs, spectra_ref, shots)
    out_ref[0, 8 : 8 + local, :] = main
    out_ref[0, 0:8, :] = edge


def source_specs(local, sources, parts, chunk, chunks, f_of):
    pieces = parts if chunks > 1 else 1
    width = sources // (pieces * chunks)

    def column(piece):
        return piece * chunks + chunk

    operator_specs = [
        pl.BlockSpec((1, 2, local, width), lambda i, c=column(p): (f_of(i), 0, 0, c))
        for p in range(pieces)
    ]
    edge_specs = [
        pl.BlockSpec((1, 16, width), lambda i, c=column(p): (f_of(i), 0, c))
        for p in range(pieces)
    ]
    return pieces, operator_specs, edge_specs


def partial_product(operator, edge, spectra, shots, chunk, chunks):
    freq_count, _, local, sources = operator.shape
    parts, _, mine, lanes = spectra.shape
    pieces, operator_specs, edge_specs = source_specs(
        local, sources, parts, chunk, chunks, lambda i: i
    )
    return pl.pallas_call(
        functools.partial(partial_kernel, shots, pieces),
        out_shape=jax.ShapeDtypeStruct((freq_count, local + 8, lanes), jnp.float32),
        grid=(freq_count,),
        in_specs=operator_specs
        + edge_specs
        + [pl.BlockSpec((parts, 1, mine, lanes), lambda i: (0, i, 0, 0))],
        out_specs=pl.BlockSpec((1, local + 8, lanes), lambda i: (i, 0, 0)),
        compiler_params=pltpu.CompilerParams(
            vmem_limit_bytes=VMEM_LIMIT, dimension_semantics=("arbitrary",)
        ),
        cost_estimate=pl.CostEstimate(
            flops=4 * freq_count * local * (sources // chunks) * lanes,
            bytes_accessed=4 * freq_count * local * (sources // chunks),
            transcendentals=0,
        ),
    )(*([operator] * pieces), *([edge] * pieces), spectra)


def adapt_kernel(freq_count, shots, points, pieces, partials, *refs):
    near_ref, operator_refs, edge_refs = refs[0], refs[1 : 1 + pieces], refs[1 + pieces : 1 + 2 * pieces]
    spectra_ref = refs[1 + 2 * pieces]
    partial_refs = refs[2 + 2 * pieces : 2 + 2 * pieces + partials]
    basis_ref, traces_ref, out_ref, predicted, lines, split_basis = refs[2 + 2 * pieces + partials :]
    step = pl.program_id(0)
    local = operator_refs[0].shape[2]
    lanes = 2 * shots
    terms = 2 * freq_count

    @pl.when(step == 0)
    def _():
        basis = basis_ref[...]
        high = basis.astype(jnp.bfloat16)
        split_basis[0:terms, :] = high
        split_basis[terms : 2 * terms, :] = high
        split_basis[2 * terms :, :] = (basis - high.astype(jnp.float32)).astype(jnp.bfloat16)

    @pl.when(step < freq_count)
    def _():
        main, edge = products(operator_refs, edge_refs, spectra_ref, shots)
        for ref in partial_refs:
            main = main + ref[0, 8 : 8 + local, :]
            edge = edge + ref[0, 0:8, :]
        predicted[step, 8 : 8 + local, :] = main
        predicted[step, 0:8, :] = edge

    @pl.when(step == freq_count - 1)
    def _():
        for f in range(freq_count):
            mine = predicted[f, 8 : 8 + local, :]
            lines[pl.ds(HALO * freq_count + f, local, stride=freq_count), :] = mine
            for h in range(HALO):
                before = h * freq_count + f
                lines[before : before + 1, :] = predicted[f, h : h + 1, :]
                after = (HALO + local + h) * freq_count + f
                lines[after : after + 1, :] = predicted[f, HALO + h : HALO + h + 1, :]

    @pl.when(step >= freq_count)
    def _():
        start = (step - freq_count) * points
        low = lax.broadcasted_iota(jnp.int32, (freq_count, lanes), 1) < shots

        def mixed(point):
            own = pl.multiple_of((point + HALO) * freq_count, freq_count)
            other = pl.multiple_of((point + HALO + near_ref[point]) * freq_count, freq_count)
            return lines[pl.ds(own, freq_count), :] + 0.5 * lines[pl.ds(other, freq_count), :]

        group = 8
        for part in range(points // group):
            reals, imags = [], []
            for pair in range(group // 2):
                first = mixed(start + part * group + 2 * pair)
                second = mixed(start + part * group + 2 * pair + 1)
                reals.append(jnp.where(low, first, swap_halves(second, shots)))
                imags.append(jnp.where(low, swap_halves(first, shots), second))
            terms_by_row = jnp.concatenate(
                [jnp.concatenate(reals, axis=1), jnp.concatenate(imags, axis=1)], axis=0
            )
            high = terms_by_row.astype(jnp.bfloat16)
            rest = (terms_by_row - high.astype(jnp.float32)).astype(jnp.bfloat16)
            left = jnp.concatenate([high, rest, high], axis=0)
            adapted = lax.dot_general(
                left, split_basis[...], TN_DIMS, preferred_element_type=jnp.float32
            )
            rows = slice(part * group * shots, (part + 1) * group * shots)
            out_ref[rows, :] = (traces_ref[rows, :].astype(jnp.float32) - adapted).astype(
                out_ref.dtype
            )


def adapt(near, operator, edge, spectra, partial, basis, traces2, shots, points, chunk, chunks):
    freq_count, _, local, sources = operator.shape
    rows, samples = traces2.shape
    parts, _, mine, lanes = spectra.shape
    block = points * shots

    def f_of(i):
        return jnp.minimum(i, freq_count - 1)

    def row_of(i):
        return jnp.maximum(i - freq_count, 0)

    pieces, operator_specs, edge_specs = source_specs(local, sources, parts, chunk, chunks, f_of)
    partial_specs = [
        pl.BlockSpec((1, local + 8, lanes), lambda i: (f_of(i), 0, 0)) for _ in partial
    ]
    return pl.pallas_call(
        functools.partial(adapt_kernel, freq_count, shots, points, pieces, len(partial)),
        out_shape=jax.ShapeDtypeStruct((rows, samples), jnp.bfloat16),
        grid=(freq_count + local // points,),
        in_specs=[pl.BlockSpec(memory_space=pltpu.SMEM)]
        + operator_specs
        + edge_specs
        + [pl.BlockSpec((parts, 1, mine, lanes), lambda i: (0, f_of(i), 0, 0))]
        + partial_specs
        + [
            pl.BlockSpec((2 * freq_count, samples), lambda i: (0, 0)),
            pl.BlockSpec((block, samples), lambda i: (row_of(i), 0)),
        ],
        out_specs=pl.BlockSpec((block, samples), lambda i: (row_of(i), 0)),
        scratch_shapes=[
            pltpu.VMEM((freq_count, local + 8, lanes), jnp.float32),
            pltpu.VMEM(((local + 2 * HALO) * freq_count, lanes), jnp.float32),
            pltpu.VMEM((6 * freq_count, samples), jnp.bfloat16),
        ],
        compiler_params=pltpu.CompilerParams(
            vmem_limit_bytes=VMEM_LIMIT, dimension_semantics=("arbitrary",)
        ),
    )(near, *([operator] * pieces), *([edge] * pieces), spectra, *partial, basis, traces2)


MESH = pl.DeviceIdType.MESH
BF16_LANES = 128


def place(size):
    me = lax.axis_index("surf")
    chips = size // 2
    chip, core = me // 2, me % 2
    position = jnp.where(chip % 2 == 0, chip // 2, chips - 1 - chip // 2)
    return me, core, position, 1 - 2 * core


def device_at(position, core, chips):
    position = (position + chips) % chips
    chip = jnp.where(position < chips // 2, 2 * position, 2 * (chips - 1 - position) + 1)
    return 2 * chip + core


def filter_basis(table, lengths, coefficients, freq_count, out):
    terms, samples = table.shape
    windows = coefficients.shape[0]
    half_taps = (TAPS - 1) // 2
    sample = lax.broadcasted_iota(jnp.int32, (1, samples), 1)
    window, end = jnp.zeros((1, samples), jnp.int32), 0
    for j in range(windows):
        end = end + lengths[j]
        window = window + jnp.where(sample >= end, 1, 0)
    member = lax.broadcasted_iota(jnp.int32, (windows, samples), 0) == window
    per_sample = lax.dot_general(
        coefficients[...],
        jnp.where(member, 1.0, 0.0),
        TN_DIMS,
        precision=lax.Precision.HIGHEST,
        preferred_element_type=jnp.float32,
    )
    base = (2.0 * freq_count * samples) ** (-0.5) * table[...]
    column = lax.broadcasted_iota(jnp.int32, (terms, samples), 1)
    basis = jnp.zeros((terms, samples), jnp.float32)
    for lag_index in range(TAPS):
        shift = lag_index - half_taps
        moved = base if shift == 0 else pltpu.roll(base, (-shift) % samples, axis=1)
        inside = (column + shift >= 0) & (column + shift < samples)
        basis = basis + per_sample[lag_index : lag_index + 1] * jnp.where(inside, moved, 0.0)
    high = basis.astype(jnp.bfloat16)
    out[0:terms, :] = high
    out[terms : 2 * terms, :] = high
    out[2 * terms :, :] = (basis - high.astype(jnp.float32)).astype(jnp.bfloat16)


def predict_kernel(
    size, freq_count, shots, local, points, subs, *refs
):
    traces, angles_table, operator, lengths, coefficients, held, lines, basis_out = refs[:8]
    table, held_sem, planes, planes_sem, spectra, total, rows = refs[8:15]
    edge_out, edge_in = refs[15:17]
    ring_send, ring_recv, pair_send, pair_recv, edge_send, edge_recv = refs[17:]
    chips = size // 2
    lanes = 2 * shots
    me, core, position, toward = place(size)
    pair = me + 1 - 2 * core
    after = device_at(position + toward, core, chips)
    before = device_at(position - toward, core, chips)
    beside = (me + 2 * core - 1 + size) % size
    tiles = local // BF16_LANES
    chunks = local // points
    sub_points = local // subs
    per_sub = chunks // subs
    slots = planes.shape[0]
    early = min(slots, chunks)
    block_rows = points * shots

    def origin(step, which):
        sign = toward * (1 - 2 * which)
        return device_at(position - step * sign, core + which - 2 * core * which, chips)

    def held_rows(chunk):
        return pl.ds(pl.multiple_of(chunk * block_rows, block_rows), block_rows)

    def held_copy(chunk):
        at = held_rows(chunk)
        return pltpu.make_async_copy(traces.at[at], held.at[at], held_sem.at[chunk])

    def fetch_planes(order):
        dev, slot = origin(order // 2, order % 2), order % slots

        def one(f, carry):
            for tile in range(tiles):
                pltpu.make_async_copy(
                    operator.at[:, f, dev * tiles + tile], planes.at[slot, f, tile], planes_sem.at[slot]
                ).start()
            return carry

        lax.fori_loop(0, freq_count, one, 0)

    def part(dev, sub):
        return spectra.at[dev, :, pl.ds(pl.multiple_of(sub * sub_points, sub_points), sub_points), :]

    def ring_copy(step, sub):
        ref = part(origin(step, 0), sub)
        return pltpu.make_async_remote_copy(
            ref, ref, ring_send.at[step, sub], ring_recv.at[step + 1, sub],
            device_id={"surf": after}, device_id_type=MESH,
        )

    def pair_copy(step, sub):
        ref = part(origin(step, 0), sub)
        return pltpu.make_async_remote_copy(
            ref, ref, pair_send.at[step, sub], pair_recv.at[step, sub],
            device_id={"surf": pair}, device_id_type=MESH,
        )

    def arrive(step, sub):
        ref = part(origin(step, 0), sub)
        pltpu.make_async_remote_copy(
            ref, ref, ring_send.at[step - 1, sub], ring_recv.at[step, sub],
            device_id={"surf": after}, device_id_type=MESH,
        ).wait_recv()

    def arrive_pair(step, sub):
        ref = part(origin(step, 1), sub)
        pltpu.make_async_remote_copy(
            ref, ref, pair_send.at[step, sub], pair_recv.at[step, sub],
            device_id={"surf": pair}, device_id_type=MESH,
        ).wait_recv()

    def product(order):
        dev = origin(order // 2, order % 2)
        slot = order % slots
        block = planes.at[slot]
        pltpu.make_async_copy(block, block, planes_sem.at[slot]).wait()
        flat = planes.reshape(slots, freq_count, tiles, 2 * local, BF16_LANES)
        for f in range(freq_count):
            left = jnp.concatenate([flat[slot, f, tile] for tile in range(tiles)], axis=1)
            total[f] += jnp.dot(left, spectra[dev, f], preferred_element_type=jnp.float32)

        @pl.when(order + early < size)
        def _():
            fetch_planes(order + early)

    def begin(chunk, carry):
        held_copy(chunk).start()
        return carry

    lax.fori_loop(0, chunks, begin, 0)

    barrier = pltpu.get_barrier_semaphore()
    for other in (after, before, pair, beside):
        pl.semaphore_signal(barrier, inc=1, device_id={"surf": other}, device_id_type=MESH)
    table[...] = angles_table[...].astype(table.dtype)
    total[...] = jnp.zeros_like(total)

    low = lax.broadcasted_iota(jnp.int32, (freq_count, lanes), 1) < shots

    def forward(chunk, carry):
        @pl.when(chunk >= chunks - early)
        def _():
            fetch_planes(chunk - (chunks - early))

        held_copy(chunk).wait()
        found = lax.dot_general(
            table[...], held[held_rows(chunk), :], NT_DIMS, preferred_element_type=jnp.float32
        )
        for two in range(points // 2):
            cols = slice(two * lanes, (two + 1) * lanes)
            real, imag = found[:freq_count, cols], found[freq_count:, cols]
            first = jnp.where(low, real, swap_halves(imag, shots))
            second = jnp.where(low, swap_halves(real, shots), imag)
            at = 2 * two * freq_count
            rows[at : at + freq_count, :] = first
            rows[at + freq_count : at + 2 * freq_count, :] = second
        start = pl.multiple_of(chunk * points, points)
        for f in range(freq_count):
            spectra[me, f, pl.ds(start, points), :] = rows[
                pl.ds(f, points, stride=freq_count), :
            ].astype(spectra.dtype)
        return carry

    for sub in range(subs):
        lax.fori_loop(sub * per_sub, (sub + 1) * per_sub, forward, 0)
        if sub == 0:
            pl.semaphore_wait(barrier, 4)
        for older in range(sub, -1, -1):
            step = sub - older
            if step <= chips - 1:
                if step > 0:
                    arrive(step, older)
                if step < chips - 1:
                    ring_copy(step, older).start()
                pair_copy(step, older).start()

    def both(step):
        product(2 * step)
        for sub in range(subs):
            arrive_pair(step, sub)
        product(2 * step + 1)

    def onward(front, carry):
        both(front - subs)
        for sub in range(subs - 1, -1, -1):
            step = front - sub

            @pl.when(step <= chips - 1)
            def _():
                arrive(step, sub)

                @pl.when(step < chips - 1)
                def _():
                    ring_copy(step, sub).start()

                pair_copy(step, sub).start()

        return carry

    filter_basis(angles_table, lengths, coefficients, freq_count, basis_out)
    lax.fori_loop(subs, chips + subs - 1, onward, 0)
    both(chips - 1)

    width = HALO * freq_count

    def combine(f, first, count):
        real = total[f, pl.ds(2 * first, count, stride=2), :]
        imag = total[f, pl.ds(2 * first + 1, count, stride=2), :]
        left_half = lax.broadcasted_iota(jnp.int32, (count, lanes), 1) < shots
        return real + jnp.where(left_half, -1.0, 1.0) * swap_halves(imag, shots)

    for f in range(freq_count):
        edge_out[0, pl.ds(f, HALO, stride=freq_count), :] = combine(f, 0, 8)[:HALO]
        edge_out[1, pl.ds(f, HALO, stride=freq_count), :] = combine(f, local - 8, 8)[8 - HALO :]

    def edge_copy(which, to):
        return pltpu.make_async_remote_copy(
            edge_out.at[which], edge_in.at[1 - which], edge_send.at[which], edge_recv.at[1 - which],
            device_id={"surf": to}, device_id_type=MESH,
        )

    previous, following = (me + size - 1) % size, (me + 1) % size
    edges = [edge_copy(0, previous), edge_copy(1, following)]
    for copy in edges:
        copy.start()
    for f in range(freq_count):
        lines[pl.ds(width + f, local, stride=freq_count), :] = combine(f, 0, local)
    for copy in edges:
        copy.wait()
    lines[0:width, :] = jnp.where(me > 0, edge_in[0], 0.0)
    lines[width + local * freq_count :, :] = jnp.where(me < size - 1, edge_in[1], 0.0)

    def drain(step, carry):
        for sub in range(subs):
            @pl.when(step < chips - 1)
            def _():
                ring_copy(step, sub).wait_send()

            pair_copy(step, sub).wait_send()
        return carry

    lax.fori_loop(0, chips, drain, 0)


def predict(
    traces2, table, operator, win_lengths, coefficients, freq_count, shots, local, size, points, subs
):
    rows, samples = traces2.shape
    sources = operator.shape[3]
    lanes = 2 * shots
    tiles = sources // BF16_LANES
    tiled = operator.reshape(local, freq_count, 2, tiles, BF16_LANES).transpose(0, 1, 3, 2, 4)
    chips = size // 2
    slots = 6
    width = HALO * freq_count
    return pl.pallas_call(
        functools.partial(predict_kernel, size, freq_count, shots, local, points, subs),
        out_shape=[
            pltpu.VMEM((rows, samples), jnp.bfloat16),
            jax.ShapeDtypeStruct(((local + 2 * HALO) * freq_count, lanes), jnp.float32),
            jax.ShapeDtypeStruct((6 * freq_count, samples), jnp.bfloat16),
        ],
        in_specs=[
            pl.BlockSpec(memory_space=pl.ANY),
            pl.BlockSpec(memory_space=pltpu.VMEM),
            pl.BlockSpec(memory_space=pl.ANY),
            pl.BlockSpec(memory_space=pltpu.SMEM),
            pl.BlockSpec(memory_space=pltpu.VMEM),
        ],
        out_specs=[pl.BlockSpec(memory_space=pltpu.VMEM)] * 3,
        scratch_shapes=[
            pltpu.VMEM((2 * freq_count, samples), jnp.bfloat16),
            pltpu.SemaphoreType.DMA((local // points,)),
            pltpu.VMEM((slots, freq_count, local // BF16_LANES, local, 2, BF16_LANES), jnp.bfloat16),
            pltpu.SemaphoreType.DMA((slots,)),
            pltpu.VMEM((size, freq_count, local, lanes), jnp.bfloat16),
            pltpu.VMEM((freq_count, 2 * local, lanes), jnp.float32),
            pltpu.VMEM((points * freq_count, lanes), jnp.float32),
            pltpu.VMEM((2, width, lanes), jnp.float32),
            pltpu.VMEM((2, width, lanes), jnp.float32),
            pltpu.SemaphoreType.DMA((chips, subs)),
            pltpu.SemaphoreType.DMA((chips, subs)),
            pltpu.SemaphoreType.DMA((chips, subs)),
            pltpu.SemaphoreType.DMA((chips, subs)),
            pltpu.SemaphoreType.DMA((2,)),
            pltpu.SemaphoreType.DMA((2,)),
        ],
        compiler_params=pltpu.CompilerParams(
            vmem_limit_bytes=PREDICT_VMEM, collective_id=0, has_side_effects=True
        ),
        cost_estimate=pl.CostEstimate(
            flops=8 * freq_count * local * sources * lanes,
            bytes_accessed=2 * rows * samples + 4 * freq_count * local * sources,
            transcendentals=0,
        ),
    )(traces2, table, tiled, win_lengths, coefficients)


def finish_kernel(freq_count, shots, points, near_ref, lines, basis, traces_ref, out_ref):
    step = pl.program_id(0)
    lanes = 2 * shots
    start = step * points
    low = lax.broadcasted_iota(jnp.int32, (freq_count, lanes), 1) < shots

    def mixed(point):
        own = pl.multiple_of((point + HALO) * freq_count, freq_count)
        other = pl.multiple_of((point + HALO + near_ref[point]) * freq_count, freq_count)
        return lines[pl.ds(own, freq_count), :] + 0.5 * lines[pl.ds(other, freq_count), :]

    group = 8
    for part in range(points // group):
        reals, imags = [], []
        for two in range(group // 2):
            first = mixed(start + part * group + 2 * two)
            second = mixed(start + part * group + 2 * two + 1)
            reals.append(jnp.where(low, first, swap_halves(second, shots)))
            imags.append(jnp.where(low, swap_halves(first, shots), second))
        terms_by_row = jnp.concatenate(
            [jnp.concatenate(reals, axis=1), jnp.concatenate(imags, axis=1)], axis=0
        )
        high = terms_by_row.astype(jnp.bfloat16)
        rest = (terms_by_row - high.astype(jnp.float32)).astype(jnp.bfloat16)
        left = jnp.concatenate([high, rest, high], axis=0)
        adapted = lax.dot_general(
            left, basis[...], TN_DIMS, preferred_element_type=jnp.float32
        )
        rows = slice(part * group * shots, (part + 1) * group * shots)
        held = pl.ds(pl.multiple_of((start + part * group) * shots, group * shots), group * shots)
        out_ref[rows, :] = (traces_ref[held, :].astype(jnp.float32) - adapted).astype(out_ref.dtype)


def finish(near, lines, basis, traces2, freq_count, shots, local, points):
    rows, samples = traces2.shape
    block = points * shots
    return pl.pallas_call(
        functools.partial(finish_kernel, freq_count, shots, points),
        out_shape=jax.ShapeDtypeStruct((rows, samples), jnp.bfloat16),
        grid=(local // points,),
        in_specs=[
            pl.BlockSpec(memory_space=pltpu.SMEM),
            pl.BlockSpec(memory_space=pltpu.VMEM),
            pl.BlockSpec(basis.shape, lambda i: (0, 0)),
            pl.BlockSpec(memory_space=pltpu.VMEM),
        ],
        out_specs=pl.BlockSpec((block, samples), lambda i: (i, 0)),
        compiler_params=pltpu.CompilerParams(
            vmem_limit_bytes=FINISH_VMEM, dimension_semantics=("arbitrary",)
        ),
        cost_estimate=pl.CostEstimate(
            flops=12 * freq_count * rows * samples, bytes_accessed=4 * rows * samples, transcendentals=0
        ),
    )(near, lines, basis, traces2)


def on_device(traces, operator, freq_bins, win_lengths, coefficients, neighbour):
    local, shots, samples = traces.shape
    freq_count = freq_bins.shape[0]
    size = lax.axis_size("surf")
    points = 32
    angles = angle_grid(freq_bins, samples)
    table = jnp.concatenate([jnp.cos(angles.T), -jnp.sin(angles.T)], axis=0)
    traces2 = traces.reshape(local * shots, samples)
    subs, step_points = 4, 16
    if size % 4 == 0 and local % (2 * BF16_LANES) == 0:
        held, lines, basis = predict(
            traces2, table, operator, win_lengths, coefficients,
            freq_count, shots, local, size, step_points, subs,
        )
        held = pltpu.with_memory_space_constraint(held, pltpu.VMEM)
        out = finish(neighbour, lines, basis, held, freq_count, shots, local, points)
        return out.reshape(local, shots, samples)

    norm = (2.0 * freq_count * samples) ** (-0.5)
    basis = matching(norm * table, coefficients, win_lengths)
    bf16_table = table.astype(jnp.bfloat16)
    up = [(i, i + 1) for i in range(size - 1)]
    down = [(j, i) for i, j in up]
    before = lax.ppermute(operator[local - HALO :], "surf", up)
    after = lax.ppermute(operator[:HALO], "surf", down)
    edge = jnp.concatenate([before, after], axis=0).transpose(1, 2, 0, 3)
    edge = jnp.pad(edge, ((0, 0), (0, 0), (0, 8 - 2 * HALO), (0, 0)))
    edge = edge.reshape(freq_count, 16, operator.shape[3])

    chunks = 1
    gathered = []
    for chunk in range(chunks):
        spectra = forward(traces2, bf16_table, freq_count, shots, points, chunk, chunks)
        gathered.append(lax.all_gather(spectra, "surf"))
    by_freq = operator.transpose(1, 2, 0, 3)
    partial = []
    for chunk in range(chunks - 1):
        partial.append(partial_product(by_freq, edge, gathered[chunk], shots, chunk, chunks))
    out = adapt(
        neighbour, by_freq, edge, gathered[-1], partial, basis, traces2,
        shots, points, chunks - 1, chunks,
    )
    return out.reshape(local, shots, samples)


def solution(mesh):
    return jax.shard_map(
        on_device,
        mesh=mesh,
        in_specs=(P("surf", "group", None), P("surf", None, None, None), P(), P(), P(), P("surf")),
        out_specs=P("surf", "group", None),
        check_vma=False,
    )
```

```python
import functools
import math

import jax
import jax.numpy as jnp
from jax import lax
from jax.experimental import pallas as pl
from jax.experimental.pallas import tpu as pltpu
from jax.sharding import PartitionSpec as P

TAPS = 31
HALO = 2
VMEM_LIMIT = 60 * 1024 * 1024
PREDICT_VMEM = 27 * 1024 * 1024
FINISH_VMEM = 24 * 1024 * 1024
NT_DIMS = (((1,), (1,)), ((), ()))
TN_DIMS = (((0,), (0,)), ((), ()))


def angle_grid(freq_bins, samples):
    sample_index = jnp.arange(samples, dtype=jnp.int32)
    phases = sample_index[:, None] * freq_bins[None, :] % samples
    return 2.0 * math.pi / samples * phases.astype(jnp.float32)


def matching(multiple_estimate, coefficients, win_lengths):
    samples = multiple_estimate.shape[1]
    half_taps = (TAPS - 1) // 2
    order = jnp.arange(win_lengths.shape[0], dtype=jnp.int32)
    window_ends = jnp.sum(jnp.where(order[:, None] <= order[None, :], win_lengths[:, None], 0), axis=0)
    sample_index = jnp.arange(samples, dtype=jnp.int32)
    window = jnp.sum((window_ends[None, :] <= sample_index[:, None]).astype(jnp.int32), axis=1)
    membership = (
        window[None, :] == jnp.arange(coefficients.shape[0], dtype=jnp.int32)[:, None]
    ).astype(jnp.float32)
    per_sample = jnp.dot(coefficients.T, membership, precision=lax.Precision.HIGHEST)
    padded = jnp.pad(multiple_estimate, ((0, 0), (half_taps, half_taps)))
    summed = jnp.zeros_like(multiple_estimate)
    for lag_index in range(TAPS):
        summed = summed + per_sample[lag_index][None] * padded[:, lag_index : lag_index + samples]
    return summed


def swap_halves(x, half):
    return pltpu.roll(x, half, axis=1)


def forward_kernel(freq_count, shots, traces_ref, table_ref, out_ref, lines):
    points = out_ref.shape[1]
    lanes = 2 * shots
    spectra = lax.dot_general(
        table_ref[...], traces_ref[...], NT_DIMS, preferred_element_type=jnp.float32
    )
    low = lax.broadcasted_iota(jnp.int32, (freq_count, lanes), 1) < shots
    for pair in range(points // 2):
        cols = slice(pair * lanes, (pair + 1) * lanes)
        real, imag = spectra[:freq_count, cols], spectra[freq_count:, cols]
        first = jnp.where(low, real, swap_halves(imag, shots))
        second = jnp.where(low, swap_halves(real, shots), imag)
        at = 2 * pair * freq_count
        lines[at : at + freq_count, :] = first
        lines[at + freq_count : at + 2 * freq_count, :] = second
    for f in range(freq_count):
        out_ref[f] = lines[pl.ds(f, points, stride=freq_count), :].astype(out_ref.dtype)


def forward(traces2, table, freq_count, shots, points, chunk, chunks):
    rows, samples = traces2.shape
    rows = rows // chunks
    local = rows // shots
    first = chunk * (local // points)
    return pl.pallas_call(
        functools.partial(forward_kernel, freq_count, shots),
        out_shape=jax.ShapeDtypeStruct((freq_count, local, 2 * shots), jnp.bfloat16),
        grid=(local // points,),
        in_specs=[
            pl.BlockSpec((points * shots, samples), lambda i: (first + i, 0)),
            pl.BlockSpec((2 * freq_count, samples), lambda i: (0, 0)),
        ],
        out_specs=pl.BlockSpec((freq_count, points, 2 * shots), lambda i: (0, i, 0)),
        scratch_shapes=[pltpu.VMEM((points * freq_count, 2 * shots), jnp.float32)],
        compiler_params=pltpu.CompilerParams(
            vmem_limit_bytes=VMEM_LIMIT, dimension_semantics=("arbitrary",)
        ),
        cost_estimate=pl.CostEstimate(
            flops=4 * freq_count * rows * samples,
            bytes_accessed=2 * rows * samples,
            transcendentals=0,
        ),
    )(traces2, table)


def combined(real_rows, imag_rows, shots):
    low = lax.broadcasted_iota(jnp.int32, real_rows.shape, 1) < shots
    return real_rows + jnp.where(low, -1.0, 1.0) * swap_halves(imag_rows, shots)


def products(operator_refs, edge_refs, spectra_ref, shots):
    spectra = spectra_ref[:, 0].reshape(-1, 2 * shots)
    planes = [
        jnp.concatenate([ref[0, part] for ref in operator_refs], axis=1) for part in range(2)
    ]
    planes.append(jnp.concatenate([ref[0] for ref in edge_refs], axis=1))
    real, imag, edge = [
        jnp.dot(plane, spectra, preferred_element_type=jnp.float32) for plane in planes
    ]
    return combined(real, imag, shots), combined(edge[0:8], edge[8:16], shots)


def partial_kernel(shots, pieces, *refs):
    operator_refs, edge_refs = refs[:pieces], refs[pieces : 2 * pieces]
    spectra_ref, out_ref = refs[2 * pieces :]
    local = operator_refs[0].shape[2]
    main, edge = products(operator_refs, edge_refs, spectra_ref, shots)
    out_ref[0, 8 : 8 + local, :] = main
    out_ref[0, 0:8, :] = edge


def source_specs(local, sources, parts, chunk, chunks, f_of):
    pieces = parts if chunks > 1 else 1
    width = sources // (pieces * chunks)

    def column(piece):
        return piece * chunks + chunk

    operator_specs = [
        pl.BlockSpec((1, 2, local, width), lambda i, c=column(p): (f_of(i), 0, 0, c))
        for p in range(pieces)
    ]
    edge_specs = [
        pl.BlockSpec((1, 16, width), lambda i, c=column(p): (f_of(i), 0, c))
        for p in range(pieces)
    ]
    return pieces, operator_specs, edge_specs


def partial_product(operator, edge, spectra, shots, chunk, chunks):
    freq_count, _, local, sources = operator.shape
    parts, _, mine, lanes = spectra.shape
    pieces, operator_specs, edge_specs = source_specs(
        local, sources, parts, chunk, chunks, lambda i: i
    )
    return pl.pallas_call(
        functools.partial(partial_kernel, shots, pieces),
        out_shape=jax.ShapeDtypeStruct((freq_count, local + 8, lanes), jnp.float32),
        grid=(freq_count,),
        in_specs=operator_specs
        + edge_specs
        + [pl.BlockSpec((parts, 1, mine, lanes), lambda i: (0, i, 0, 0))],
        out_specs=pl.BlockSpec((1, local + 8, lanes), lambda i: (i, 0, 0)),
        compiler_params=pltpu.CompilerParams(
            vmem_limit_bytes=VMEM_LIMIT, dimension_semantics=("arbitrary",)
        ),
        cost_estimate=pl.CostEstimate(
            flops=4 * freq_count * local * (sources // chunks) * lanes,
            bytes_accessed=4 * freq_count * local * (sources // chunks),
            transcendentals=0,
        ),
    )(*([operator] * pieces), *([edge] * pieces), spectra)


def adapt_kernel(freq_count, shots, points, pieces, partials, *refs):
    near_ref, operator_refs, edge_refs = refs[0], refs[1 : 1 + pieces], refs[1 + pieces : 1 + 2 * pieces]
    spectra_ref = refs[1 + 2 * pieces]
    partial_refs = refs[2 + 2 * pieces : 2 + 2 * pieces + partials]
    basis_ref, traces_ref, out_ref, predicted, lines, split_basis = refs[2 + 2 * pieces + partials :]
    step = pl.program_id(0)
    local = operator_refs[0].shape[2]
    lanes = 2 * shots
    terms = 2 * freq_count

    @pl.when(step == 0)
    def _():
        basis = basis_ref[...]
        high = basis.astype(jnp.bfloat16)
        split_basis[0:terms, :] = high
        split_basis[terms : 2 * terms, :] = high
        split_basis[2 * terms :, :] = (basis - high.astype(jnp.float32)).astype(jnp.bfloat16)

    @pl.when(step < freq_count)
    def _():
        main, edge = products(operator_refs, edge_refs, spectra_ref, shots)
        for ref in partial_refs:
            main = main + ref[0, 8 : 8 + local, :]
            edge = edge + ref[0, 0:8, :]
        predicted[step, 8 : 8 + local, :] = main
        predicted[step, 0:8, :] = edge

    @pl.when(step == freq_count - 1)
    def _():
        for f in range(freq_count):
            mine = predicted[f, 8 : 8 + local, :]
            lines[pl.ds(HALO * freq_count + f, local, stride=freq_count), :] = mine
            for h in range(HALO):
                before = h * freq_count + f
                lines[before : before + 1, :] = predicted[f, h : h + 1, :]
                after = (HALO + local + h) * freq_count + f
                lines[after : after + 1, :] = predicted[f, HALO + h : HALO + h + 1, :]

    @pl.when(step >= freq_count)
    def _():
        start = (step - freq_count) * points
        low = lax.broadcasted_iota(jnp.int32, (freq_count, lanes), 1) < shots

        def mixed(point):
            own = pl.multiple_of((point + HALO) * freq_count, freq_count)
            other = pl.multiple_of((point + HALO + near_ref[point]) * freq_count, freq_count)
            return lines[pl.ds(own, freq_count), :] + 0.5 * lines[pl.ds(other, freq_count), :]

        group = 8
        for part in range(points // group):
            reals, imags = [], []
            for pair in range(group // 2):
                first = mixed(start + part * group + 2 * pair)
                second = mixed(start + part * group + 2 * pair + 1)
                reals.append(jnp.where(low, first, swap_halves(second, shots)))
                imags.append(jnp.where(low, swap_halves(first, shots), second))
            terms_by_row = jnp.concatenate(
                [jnp.concatenate(reals, axis=1), jnp.concatenate(imags, axis=1)], axis=0
            )
            high = terms_by_row.astype(jnp.bfloat16)
            rest = (terms_by_row - high.astype(jnp.float32)).astype(jnp.bfloat16)
            left = jnp.concatenate([high, rest, high], axis=0)
            adapted = lax.dot_general(
                left, split_basis[...], TN_DIMS, preferred_element_type=jnp.float32
            )
            rows = slice(part * group * shots, (part + 1) * group * shots)
            out_ref[rows, :] = (traces_ref[rows, :].astype(jnp.float32) - adapted).astype(
                out_ref.dtype
            )


def adapt(near, operator, edge, spectra, partial, basis, traces2, shots, points, chunk, chunks):
    freq_count, _, local, sources = operator.shape
    rows, samples = traces2.shape
    parts, _, mine, lanes = spectra.shape
    block = points * shots

    def f_of(i):
        return jnp.minimum(i, freq_count - 1)

    def row_of(i):
        return jnp.maximum(i - freq_count, 0)

    pieces, operator_specs, edge_specs = source_specs(local, sources, parts, chunk, chunks, f_of)
    partial_specs = [
        pl.BlockSpec((1, local + 8, lanes), lambda i: (f_of(i), 0, 0)) for _ in partial
    ]
    return pl.pallas_call(
        functools.partial(adapt_kernel, freq_count, shots, points, pieces, len(partial)),
        out_shape=jax.ShapeDtypeStruct((rows, samples), jnp.bfloat16),
        grid=(freq_count + local // points,),
        in_specs=[pl.BlockSpec(memory_space=pltpu.SMEM)]
        + operator_specs
        + edge_specs
        + [pl.BlockSpec((parts, 1, mine, lanes), lambda i: (0, f_of(i), 0, 0))]
        + partial_specs
        + [
            pl.BlockSpec((2 * freq_count, samples), lambda i: (0, 0)),
            pl.BlockSpec((block, samples), lambda i: (row_of(i), 0)),
        ],
        out_specs=pl.BlockSpec((block, samples), lambda i: (row_of(i), 0)),
        scratch_shapes=[
            pltpu.VMEM((freq_count, local + 8, lanes), jnp.float32),
            pltpu.VMEM(((local + 2 * HALO) * freq_count, lanes), jnp.float32),
            pltpu.VMEM((6 * freq_count, samples), jnp.bfloat16),
        ],
        compiler_params=pltpu.CompilerParams(
            vmem_limit_bytes=VMEM_LIMIT, dimension_semantics=("arbitrary",)
        ),
    )(near, *([operator] * pieces), *([edge] * pieces), spectra, *partial, basis, traces2)


MESH = pl.DeviceIdType.MESH
BF16_LANES = 128


def place(size):
    me = lax.axis_index("surf")
    chips = size // 2
    chip, core = me // 2, me % 2
    position = jnp.where(chip % 2 == 0, chip // 2, chips - 1 - chip // 2)
    return me, core, position, 1 - 2 * core


def device_at(position, core, chips):
    position = (position + chips) % chips
    chip = jnp.where(position < chips // 2, 2 * position, 2 * (chips - 1 - position) + 1)
    return 2 * chip + core


def filter_basis(table, lengths, coefficients, freq_count, out):
    terms, samples = table.shape
    windows = coefficients.shape[0]
    half_taps = (TAPS - 1) // 2
    sample = lax.broadcasted_iota(jnp.int32, (1, samples), 1)
    window, end = jnp.zeros((1, samples), jnp.int32), 0
    for j in range(windows):
        end = end + lengths[j]
        window = window + jnp.where(sample >= end, 1, 0)
    member = lax.broadcasted_iota(jnp.int32, (windows, samples), 0) == window
    per_sample = lax.dot_general(
        coefficients[...],
        jnp.where(member, 1.0, 0.0),
        TN_DIMS,
        precision=lax.Precision.HIGHEST,
        preferred_element_type=jnp.float32,
    )
    base = (2.0 * freq_count * samples) ** (-0.5) * table[...]
    column = lax.broadcasted_iota(jnp.int32, (terms, samples), 1)
    basis = jnp.zeros((terms, samples), jnp.float32)
    for lag_index in range(TAPS):
        shift = lag_index - half_taps
        moved = base if shift == 0 else pltpu.roll(base, (-shift) % samples, axis=1)
        inside = (column + shift >= 0) & (column + shift < samples)
        basis = basis + per_sample[lag_index : lag_index + 1] * jnp.where(inside, moved, 0.0)
    high = basis.astype(jnp.bfloat16)
    out[0:terms, :] = high
    out[terms : 2 * terms, :] = high
    out[2 * terms :, :] = (basis - high.astype(jnp.float32)).astype(jnp.bfloat16)


def predict_kernel(
    size, freq_count, shots, local, points, subs, *refs
):
    traces, angles_table, operator, lengths, coefficients, held, lines, basis_out = refs[:8]
    table, held_sem, planes, planes_sem, spectra, total, rows = refs[8:15]
    edge_out, edge_in = refs[15:17]
    ring_send, ring_recv, pair_send, pair_recv, edge_send, edge_recv = refs[17:]
    chips = size // 2
    lanes = 2 * shots
    me, core, position, toward = place(size)
    pair = me + 1 - 2 * core
    after = device_at(position + toward, core, chips)
    before = device_at(position - toward, core, chips)
    beside = (me + 2 * core - 1 + size) % size
    tiles = local // BF16_LANES
    chunks = local // points
    sub_points = local // subs
    per_sub = chunks // subs
    slots = planes.shape[0]
    early = min(slots, chunks)
    block_rows = points * shots

    def origin(step, which):
        sign = toward * (1 - 2 * which)
        return device_at(position - step * sign, core + which - 2 * core * which, chips)

    def held_rows(chunk):
        return pl.ds(pl.multiple_of(chunk * block_rows, block_rows), block_rows)

    def held_copy(chunk):
        at = held_rows(chunk)
        return pltpu.make_async_copy(traces.at[at], held.at[at], held_sem.at[chunk])

    def fetch_planes(order):
        dev, slot = origin(order // 2, order % 2), order % slots

        def one(f, carry):
            for tile in range(tiles):
                pltpu.make_async_copy(
                    operator.at[:, f, dev * tiles + tile], planes.at[slot, f, tile], planes_sem.at[slot]
                ).start()
            return carry

        lax.fori_loop(0, freq_count, one, 0)

    def part(dev, sub):
        return spectra.at[dev, :, pl.ds(pl.multiple_of(sub * sub_points, sub_points), sub_points), :]

    def ring_copy(step, sub):
        ref = part(origin(step, 0), sub)
        return pltpu.make_async_remote_copy(
            ref, ref, ring_send.at[step, sub], ring_recv.at[step + 1, sub],
            device_id={"surf": after}, device_id_type=MESH,
        )

    def pair_copy(step, sub):
        ref = part(origin(step, 0), sub)
        return pltpu.make_async_remote_copy(
            ref, ref, pair_send.at[step, sub], pair_recv.at[step, sub],
            device_id={"surf": pair}, device_id_type=MESH,
        )

    def arrive(step, sub):
        ref = part(origin(step, 0), sub)
        pltpu.make_async_remote_copy(
            ref, ref, ring_send.at[step - 1, sub], ring_recv.at[step, sub],
            device_id={"surf": after}, device_id_type=MESH,
        ).wait_recv()

    def arrive_pair(step, sub):
        ref = part(origin(step, 1), sub)
        pltpu.make_async_remote_copy(
            ref, ref, pair_send.at[step, sub], pair_recv.at[step, sub],
            device_id={"surf": pair}, device_id_type=MESH,
        ).wait_recv()

    def product(order):
        dev = origin(order // 2, order % 2)
        slot = order % slots
        block = planes.at[slot]
        pltpu.make_async_copy(block, block, planes_sem.at[slot]).wait()
        flat = planes.reshape(slots, freq_count, tiles, 2 * local, BF16_LANES)
        for f in range(freq_count):
            left = jnp.concatenate([flat[slot, f, tile] for tile in range(tiles)], axis=1)
            total[f] += jnp.dot(left, spectra[dev, f], preferred_element_type=jnp.float32)

        @pl.when(order + early < size)
        def _():
            fetch_planes(order + early)

    def begin(chunk, carry):
        held_copy(chunk).start()
        return carry

    lax.fori_loop(0, chunks, begin, 0)

    barrier = pltpu.get_barrier_semaphore()
    for other in (after, before, pair, beside):
        pl.semaphore_signal(barrier, inc=1, device_id={"surf": other}, device_id_type=MESH)
    table[...] = angles_table[...].astype(table.dtype)
    total[...] = jnp.zeros_like(total)

    low = lax.broadcasted_iota(jnp.int32, (freq_count, lanes), 1) < shots

    def forward(chunk, carry):
        @pl.when(chunk >= chunks - early)
        def _():
            fetch_planes(chunk - (chunks - early))

        held_copy(chunk).wait()
        found = lax.dot_general(
            table[...], held[held_rows(chunk), :], NT_DIMS, preferred_element_type=jnp.float32
        )
        for two in range(points // 2):
            cols = slice(two * lanes, (two + 1) * lanes)
            real, imag = found[:freq_count, cols], found[freq_count:, cols]
            first = jnp.where(low, real, swap_halves(imag, shots))
            second = jnp.where(low, swap_halves(real, shots), imag)
            at = 2 * two * freq_count
            rows[at : at + freq_count, :] = first
            rows[at + freq_count : at + 2 * freq_count, :] = second
        start = pl.multiple_of(chunk * points, points)
        for f in range(freq_count):
            spectra[me, f, pl.ds(start, points), :] = rows[
                pl.ds(f, points, stride=freq_count), :
            ].astype(spectra.dtype)
        return carry

    for sub in range(subs):
        lax.fori_loop(sub * per_sub, (sub + 1) * per_sub, forward, 0)
        if sub == 0:
            pl.semaphore_wait(barrier, 4)
        for older in range(sub, -1, -1):
            step = sub - older
            if step <= chips - 1:
                if step > 0:
                    arrive(step, older)
                if step < chips - 1:
                    ring_copy(step, older).start()
                pair_copy(step, older).start()

    def both(step):
        product(2 * step)
        for sub in range(subs):
            arrive_pair(step, sub)
        product(2 * step + 1)

    def onward(front, carry):
        for sub in range(subs - 1, -1, -1):
            step = front - sub
            if sub == subs - 2:
                both(front - subs)

            @pl.when(step <= chips - 1)
            def _():
                arrive(step, sub)

                @pl.when(step < chips - 1)
                def _():
                    ring_copy(step, sub).start()

                pair_copy(step, sub).start()

        return carry

    filter_basis(angles_table, lengths, coefficients, freq_count, basis_out)
    lax.fori_loop(subs, chips + subs - 1, onward, 0)
    both(chips - 1)

    width = HALO * freq_count

    def combine(f, first, count):
        real = total[f, pl.ds(2 * first, count, stride=2), :]
        imag = total[f, pl.ds(2 * first + 1, count, stride=2), :]
        left_half = lax.broadcasted_iota(jnp.int32, (count, lanes), 1) < shots
        return real + jnp.where(left_half, -1.0, 1.0) * swap_halves(imag, shots)

    for f in range(freq_count):
        edge_out[0, pl.ds(f, HALO, stride=freq_count), :] = combine(f, 0, 8)[:HALO]
        edge_out[1, pl.ds(f, HALO, stride=freq_count), :] = combine(f, local - 8, 8)[8 - HALO :]

    def edge_copy(which, to):
        return pltpu.make_async_remote_copy(
            edge_out.at[which], edge_in.at[1 - which], edge_send.at[which], edge_recv.at[1 - which],
            device_id={"surf": to}, device_id_type=MESH,
        )

    previous, following = (me + size - 1) % size, (me + 1) % size
    edges = [edge_copy(0, previous), edge_copy(1, following)]
    for copy in edges:
        copy.start()
    for f in range(freq_count):
        lines[pl.ds(width + f, local, stride=freq_count), :] = combine(f, 0, local)
    for copy in edges:
        copy.wait()
    lines[0:width, :] = jnp.where(me > 0, edge_in[0], 0.0)
    lines[width + local * freq_count :, :] = jnp.where(me < size - 1, edge_in[1], 0.0)

    def drain(step, carry):
        for sub in range(subs):
            @pl.when(step < chips - 1)
            def _():
                ring_copy(step, sub).wait_send()

            pair_copy(step, sub).wait_send()
        return carry

    lax.fori_loop(0, chips, drain, 0)


def predict(
    traces2, table, operator, win_lengths, coefficients, freq_count, shots, local, size, points, subs
):
    rows, samples = traces2.shape
    sources = operator.shape[3]
    lanes = 2 * shots
    tiles = sources // BF16_LANES
    tiled = operator.reshape(local, freq_count, 2, tiles, BF16_LANES).transpose(0, 1, 3, 2, 4)
    chips = size // 2
    slots = 6
    width = HALO * freq_count
    return pl.pallas_call(
        functools.partial(predict_kernel, size, freq_count, shots, local, points, subs),
        out_shape=[
            pltpu.VMEM((rows, samples), jnp.bfloat16),
            jax.ShapeDtypeStruct(((local + 2 * HALO) * freq_count, lanes), jnp.float32),
            jax.ShapeDtypeStruct((6 * freq_count, samples), jnp.bfloat16),
        ],
        in_specs=[
            pl.BlockSpec(memory_space=pl.ANY),
            pl.BlockSpec(memory_space=pltpu.VMEM),
            pl.BlockSpec(memory_space=pl.ANY),
            pl.BlockSpec(memory_space=pltpu.SMEM),
            pl.BlockSpec(memory_space=pltpu.VMEM),
        ],
        out_specs=[pl.BlockSpec(memory_space=pltpu.VMEM)] * 3,
        scratch_shapes=[
            pltpu.VMEM((2 * freq_count, samples), jnp.bfloat16),
            pltpu.SemaphoreType.DMA((local // points,)),
            pltpu.VMEM((slots, freq_count, local // BF16_LANES, local, 2, BF16_LANES), jnp.bfloat16),
            pltpu.SemaphoreType.DMA((slots,)),
            pltpu.VMEM((size, freq_count, local, lanes), jnp.bfloat16),
            pltpu.VMEM((freq_count, 2 * local, lanes), jnp.float32),
            pltpu.VMEM((points * freq_count, lanes), jnp.float32),
            pltpu.VMEM((2, width, lanes), jnp.float32),
            pltpu.VMEM((2, width, lanes), jnp.float32),
            pltpu.SemaphoreType.DMA((chips, subs)),
            pltpu.SemaphoreType.DMA((chips, subs)),
            pltpu.SemaphoreType.DMA((chips, subs)),
            pltpu.SemaphoreType.DMA((chips, subs)),
            pltpu.SemaphoreType.DMA((2,)),
            pltpu.SemaphoreType.DMA((2,)),
        ],
        compiler_params=pltpu.CompilerParams(
            vmem_limit_bytes=PREDICT_VMEM, collective_id=0, has_side_effects=True
        ),
        cost_estimate=pl.CostEstimate(
            flops=8 * freq_count * local * sources * lanes,
            bytes_accessed=2 * rows * samples + 4 * freq_count * local * sources,
            transcendentals=0,
        ),
    )(traces2, table, tiled, win_lengths, coefficients)


def finish_kernel(freq_count, shots, points, near_ref, lines, basis, traces_ref, out_ref):
    step = pl.program_id(0)
    lanes = 2 * shots
    start = step * points
    low = lax.broadcasted_iota(jnp.int32, (freq_count, lanes), 1) < shots

    def mixed(point):
        own = pl.multiple_of((point + HALO) * freq_count, freq_count)
        other = pl.multiple_of((point + HALO + near_ref[point]) * freq_count, freq_count)
        return lines[pl.ds(own, freq_count), :] + 0.5 * lines[pl.ds(other, freq_count), :]

    group = 8
    for part in range(points // group):
        reals, imags = [], []
        for two in range(group // 2):
            first = mixed(start + part * group + 2 * two)
            second = mixed(start + part * group + 2 * two + 1)
            reals.append(jnp.where(low, first, swap_halves(second, shots)))
            imags.append(jnp.where(low, swap_halves(first, shots), second))
        terms_by_row = jnp.concatenate(
            [jnp.concatenate(reals, axis=1), jnp.concatenate(imags, axis=1)], axis=0
        )
        high = terms_by_row.astype(jnp.bfloat16)
        rest = (terms_by_row - high.astype(jnp.float32)).astype(jnp.bfloat16)
        left = jnp.concatenate([high, rest, high], axis=0)
        adapted = lax.dot_general(
            left, basis[...], TN_DIMS, preferred_element_type=jnp.float32
        )
        rows = slice(part * group * shots, (part + 1) * group * shots)
        held = pl.ds(pl.multiple_of((start + part * group) * shots, group * shots), group * shots)
        out_ref[rows, :] = (traces_ref[held, :].astype(jnp.float32) - adapted).astype(out_ref.dtype)


def finish(near, lines, basis, traces2, freq_count, shots, local, points):
    rows, samples = traces2.shape
    block = points * shots
    return pl.pallas_call(
        functools.partial(finish_kernel, freq_count, shots, points),
        out_shape=jax.ShapeDtypeStruct((rows, samples), jnp.bfloat16),
        grid=(local // points,),
        in_specs=[
            pl.BlockSpec(memory_space=pltpu.SMEM),
            pl.BlockSpec(memory_space=pltpu.VMEM),
            pl.BlockSpec(basis.shape, lambda i: (0, 0)),
            pl.BlockSpec(memory_space=pltpu.VMEM),
        ],
        out_specs=pl.BlockSpec((block, samples), lambda i: (i, 0)),
        compiler_params=pltpu.CompilerParams(
            vmem_limit_bytes=FINISH_VMEM, dimension_semantics=("arbitrary",)
        ),
        cost_estimate=pl.CostEstimate(
            flops=12 * freq_count * rows * samples, bytes_accessed=4 * rows * samples, transcendentals=0
        ),
    )(near, lines, basis, traces2)


def on_device(traces, operator, freq_bins, win_lengths, coefficients, neighbour):
    local, shots, samples = traces.shape
    freq_count = freq_bins.shape[0]
    size = lax.axis_size("surf")
    points = 32
    angles = angle_grid(freq_bins, samples)
    table = jnp.concatenate([jnp.cos(angles.T), -jnp.sin(angles.T)], axis=0)
    traces2 = traces.reshape(local * shots, samples)
    subs, step_points = 4, 16
    if size % 4 == 0 and local % (2 * BF16_LANES) == 0:
        held, lines, basis = predict(
            traces2, table, operator, win_lengths, coefficients,
            freq_count, shots, local, size, step_points, subs,
        )
        held = pltpu.with_memory_space_constraint(held, pltpu.VMEM)
        out = finish(neighbour, lines, basis, held, freq_count, shots, local, points)
        return out.reshape(local, shots, samples)

    norm = (2.0 * freq_count * samples) ** (-0.5)
    basis = matching(norm * table, coefficients, win_lengths)
    bf16_table = table.astype(jnp.bfloat16)
    up = [(i, i + 1) for i in range(size - 1)]
    down = [(j, i) for i, j in up]
    before = lax.ppermute(operator[local - HALO :], "surf", up)
    after = lax.ppermute(operator[:HALO], "surf", down)
    edge = jnp.concatenate([before, after], axis=0).transpose(1, 2, 0, 3)
    edge = jnp.pad(edge, ((0, 0), (0, 0), (0, 8 - 2 * HALO), (0, 0)))
    edge = edge.reshape(freq_count, 16, operator.shape[3])

    chunks = 1
    gathered = []
    for chunk in range(chunks):
        spectra = forward(traces2, bf16_table, freq_count, shots, points, chunk, chunks)
        gathered.append(lax.all_gather(spectra, "surf"))
    by_freq = operator.transpose(1, 2, 0, 3)
    partial = []
    for chunk in range(chunks - 1):
        partial.append(partial_product(by_freq, edge, gathered[chunk], shots, chunk, chunks))
    out = adapt(
        neighbour, by_freq, edge, gathered[-1], partial, basis, traces2,
        shots, points, chunks - 1, chunks,
    )
    return out.reshape(local, shots, samples)


def solution(mesh):
    return jax.shard_map(
        on_device,
        mesh=mesh,
        in_specs=(P("surf", "group", None), P("surf", None, None, None), P(), P(), P(), P("surf")),
        out_specs=P("surf", "group", None),
        check_vma=False,
    )
```
